512 devices in a mesh: section: 16 (over y, core), expert: 32 (over x, z).
Axes of the slice: x: 4, y: 8, z: 8, core: 2. Of those that a mesh axis runs over, the one named last changes fastest.
Arguments:
- tokens: bfloat16 [16, 2048, 2560], P('section', 'expert'), may hold values from -6 to 6
- norm_gain: float32 [16, 2560], P('section'), may hold values from 0.25 to 1.75
- w_gate: bfloat16 [16, 32, 2560, 192], P('section', 'expert'), may hold values from -0.125 to 0.125
- w_up: bfloat16 [16, 32, 2560, 192], P('section', 'expert'), may hold values from -0.125 to 0.125
- w_down: bfloat16 [16, 32, 192, 2560], P('section', 'expert'), may hold values from -0.21875 to 0.21875
- routes: int32 [16, 2, 2048, 1], P('section', None, 'expert'), may hold values from 0 to 7; in each aligned block of 64 rows (0 to 63, 64 to 127, ..., all dimensions but the last counted through in order) at most 9 rows name the same one
- mix_weights: float32 [16, 2, 2048, 1], P('section', None, 'expert'), may hold values from 0.1 to 1
- cotangent: bfloat16 [16, 2048, 2560], P('section', 'expert'), may hold values from -6 to 6
Outputs:
- final: bfloat16 [16, 2048, 2560], P('section', 'expert')
- input_grads: bfloat16 [16, 2048, 2560], P('section', 'expert')
The draws below stay inside these ranges and needn't reach their ends.
Inputs may be any that keep to these rules, and one draw needn't show every extreme that they name: `routes`: the 1 ids of a token differ. In the rows of one device (aligned blocks of 64 tokens of one layer and step) no id is named by more than 9 tokens, a bound that some block reaches.
All inputs are finite; a program needn't handle non-finite values.
Results may differ from the reference program's by a relative error of at most 0.011.
Values may be sent and summed in bfloat16 or wider, within the bound.
A program may use at most 64 MiB of HBM per device.

```python
import math
import jax
import jax.numpy as jnp
import numpy as np
from jax import lax

D = 2560
HID = 768
SPLIT = 4
TOPK = 1
STEPS = 2
TOK_DEV = 64
HID_DEV = 192
LAYERS = 16
EXPERTS = 8
CAP = 9
MB_TOK = 2048
N_EXPERT = 32


def steps_of(own_key, extent, cuts, low, top_value):
    def one(axis_at, shards_of):
        draws = jax.random.uniform(jax.random.fold_in(jax.random.fold_in(own_key, 6), axis_at), (shards_of,), jnp.float32, low / len(cuts), top_value / len(cuts))
        return jnp.repeat(jnp.exp(draws), extent[axis_at] // shards_of).reshape((-1,) + (1,) * (len(extent) - axis_at - 1))

    loudness = one(*cuts[0])
    for cut in cuts[1:]:
        loudness = loudness * one(*cut)
    return loudness


def assign_block(rng, own, number, rows, number_of, top, limit, slope):
    sequence = jax.random.permutation(rng, number_of)
    heavy_load, ordinary = shares(number_of, rows * top, limit, slope, True), shares(number_of, rows * top, limit, slope, False)
    places = jnp.arange(number_of)

    def named(sizes, rotation):
        used = int((sizes > 0).sum())
        fixed = max(1, used // 4)
        passed = fixed + (places - fixed + rotation * (used - fixed)) % max(1, number_of - fixed)
        return jnp.zeros((number_of,), jnp.int32).at[sequence[jnp.where(places < fixed, places, passed)]].set(jnp.asarray(sizes, jnp.int32))

    sizes = jnp.where(number % 4 == 0, named(heavy_load, number // 4), named(ordinary, number - number // 4 - 1))
    mixed = jax.random.permutation(jax.random.fold_in(own, 3), number_of)
    giver, taker = mixed[0:number_of // 2 * 2:2], mixed[1:number_of // 2 * 2:2]
    margin = jnp.minimum(sizes[giver] - 1, limit - sizes[taker]) // 2
    margin = jnp.where((giver == sequence[0]) | (taker == sequence[0]) | (sizes[taker] == 0), 0, jnp.maximum(margin, 0))
    passed = jax.random.randint(jax.random.fold_in(own, 4), (number_of // 2,), 0, 1 << 20) % (margin + 1)
    sizes = sizes.at[giver].add(-passed).at[taker].add(passed)
    items = jnp.searchsorted(jnp.cumsum(sizes), jnp.arange(rows * top), side="right").astype(jnp.int32)
    grid = items.reshape(top, rows).T
    grid = grid[jax.random.permutation(jax.random.fold_in(own, 1), rows)]
    rotation = jax.random.randint(jax.random.fold_in(own, 2), (rows, 1), 0, top)
    return jnp.take_along_axis(grid, (jnp.arange(top)[None, :] + rotation) % top, axis=1)


def shares(number_of, total, reach, lean, full):
    weights = [(1 << 20) // math.isqrt(grade ** lean) + 1 for grade in range(1, number_of + 1)]
    largest = reach if full else min(reach, max(-(-total // number_of), total * weights[0] // sum(weights)))
    least = 1 if total - largest >= number_of - 1 else 0
    counts, rest = [largest] + [least] * (number_of - 1), total - largest - least * (number_of - 1)
    while rest > 0:
        free = [i for i in range(1, number_of) if counts[i] < largest] or [i for i in range(1, number_of) if counts[i] < reach]
        whole, left = sum([weights[i] for i in free]), rest
        for i in free:
            more = min(reach - counts[i], max(1, left * weights[i] // whole), rest)
            counts[i] = counts[i] + more
            rest = rest - more
    return np.array(counts)


def gaussian(key, dims, deviation, limit, cuts=(), held_as=jnp.bfloat16):
    factor_of = steps_of(key, dims, cuts, -0.22, 0.18) if cuts else 1.0
    array = jax.random.normal(key, dims, jnp.float32) * deviation * factor_of
    return jnp.minimum(jnp.maximum(array, -limit), limit).astype(held_as)


def setup_inputs(seed: int = 0) -> dict:
    seeds = jax.random.split(jax.random.key(seed), 9)
    tokens = gaussian(seeds[0], (LAYERS, MB_TOK, D), 1.0, 6.0, ((0, 16), (1, 32)))
    norm_gain = jnp.clip(1.0 + 0.15 * jax.random.normal(seeds[1], (LAYERS, D), jnp.float32), 0.25, 1.75)
    w_gate = gaussian(seeds[2], (LAYERS, N_EXPERT, D, HID_DEV), D ** -0.5, 0.125, ((0, 16), (1, 32)))
    w_up = gaussian(seeds[3], (LAYERS, N_EXPERT, D, HID_DEV), D ** -0.5, 0.125, ((0, 16), (1, 32)))
    w_down = gaussian(seeds[4], (LAYERS, N_EXPERT, HID_DEV, D), HID ** -0.5, 0.21875, ((0, 16), (1, 32)))
    routes_keys = jax.random.split(jax.random.fold_in(seeds[5], 1), LAYERS * STEPS * MB_TOK // TOK_DEV)
    routes_turns = jax.random.permutation(jax.random.fold_in(seeds[5], 3), LAYERS * STEPS * MB_TOK // TOK_DEV)
    routes = jax.vmap(lambda own, number: assign_block(jax.random.fold_in(seeds[5], 2), own, number, TOK_DEV, EXPERTS, TOPK, CAP, 1))(routes_keys, routes_turns).reshape((LAYERS, STEPS, MB_TOK, TOPK))
    mix_weights = jnp.clip(jnp.exp(math.log(1.0) - 2.3025851 * jax.random.uniform(seeds[6], (LAYERS, STEPS, MB_TOK, TOPK), jnp.float32) ** steps_of(seeds[6], (LAYERS, STEPS, MB_TOK, TOPK), ((0, 16), (2, 32)), -0.2, 0.2)), 0.1, 1.0)
    cotangent = gaussian(seeds[7], (LAYERS, MB_TOK, D), 1.0, 6.0, ((0, 16), (1, 32)))
    return {"tokens": tokens, "norm_gain": norm_gain, "w_gate": w_gate, "w_up": w_up, "w_down": w_down, "routes": routes, "mix_weights": mix_weights, "cotangent": cotangent}


EPSILON = 1e-06
HIGHEST = lax.Precision.HIGHEST

def norm_apply(hidden_f, gain_row):
    inv_scale = lax.rsqrt(lax.optimization_barrier(jnp.mean(hidden_f * hidden_f, axis=-1, keepdims=True)) + EPSILON)
    return hidden_f * inv_scale * gain_row

def slot_index(route_ids, experts, capacity):
    labels = jnp.arange(experts, dtype=jnp.int32)
    chosen = lax.optimization_barrier(jnp.sum((route_ids[:, :, None] == labels[None, None, :]).astype(jnp.int32), axis=1))
    before = jnp.cumsum(chosen, axis=0) - chosen
    within = jnp.take_along_axis(before, route_ids, axis=1)
    return (route_ids * capacity + within).astype(jnp.int32)

def blocks_slots(route_ids):
    return jax.vmap(lambda part_ids: slot_index(part_ids, EXPERTS, CAP))(route_ids.reshape(N_EXPERT, TOK_DEV, TOPK))

def dispatch(values, slot_ids):

    def one_block(block_values, places):
        repeated = jnp.repeat(block_values, TOPK, axis=0)
        empty = jnp.zeros((EXPERTS * CAP, block_values.shape[1]), block_values.dtype)
        return empty.at[places.reshape(-1)].set(repeated)
    send_boxes = jax.vmap(one_block)(values, slot_ids)
    return jnp.swapaxes(send_boxes.reshape(N_EXPERT, EXPERTS, CAP, values.shape[2]), 0, 1)

def collect(slot_rows, slot_ids):
    returned = jnp.swapaxes(slot_rows, 0, 1).reshape(N_EXPERT, EXPERTS * CAP, slot_rows.shape[3])
    return jax.vmap(lambda block_rows, places: block_rows[places])(returned, slot_ids)

def round_trip(values):
    return lax.optimization_barrier(values.astype(jnp.bfloat16)).astype(jnp.float32)

def split_weights(gate_w, up_w, down_w):
    gate_s = gate_w.astype(jnp.float32).reshape(EXPERTS, SPLIT, D, HID_DEV)
    up_s = up_w.astype(jnp.float32).reshape(EXPERTS, SPLIT, D, HID_DEV)
    down_s = down_w.astype(jnp.float32).reshape(EXPERTS, SPLIT, HID_DEV, D)
    return (gate_s, up_s, down_s)

def gate_up(slot_rows, gate_s, up_s):
    gate_act = jnp.einsum('enrd,esdh->esnrh', slot_rows, gate_s, precision=HIGHEST)
    upper = jnp.einsum('enrd,esdh->esnrh', slot_rows, up_s, precision=HIGHEST)
    return (gate_act, upper)

def normed_rows(hidden, gain_row):
    return norm_apply(hidden.astype(jnp.float32), gain_row).astype(jnp.bfloat16).reshape(N_EXPERT, TOK_DEV, D)

def layer_forward(hidden, gain_row, gate_w, up_w, down_w, route_ids, mix_row):
    gate_s, up_s, down_s = split_weights(gate_w, up_w, down_w)
    slot_ids = blocks_slots(route_ids)
    slot_rows = dispatch(normed_rows(hidden, gain_row), slot_ids).astype(jnp.float32)
    gate_act, upper = gate_up(slot_rows, gate_s, up_s)
    inner_act = round_trip(jax.nn.silu(gate_act) * upper)
    partial_value = round_trip(jnp.einsum('esnrh,eshd->esnrd', inner_act, down_s, precision=HIGHEST))
    outputs = round_trip(lax.optimization_barrier(jnp.sum(partial_value, axis=1)))
    picked = collect(outputs, slot_ids)
    combined = lax.optimization_barrier(jnp.sum(mix_row.reshape(N_EXPERT, TOK_DEV, TOPK)[..., None] * picked, axis=2)).reshape(MB_TOK, D)
    return (hidden.astype(jnp.float32) + combined).astype(jnp.bfloat16)

def layer_backward(hidden, grad_now, gain_row, gate_w, up_w, down_w, route_ids, mix_row):
    gate_s, up_s, down_s = split_weights(gate_w, up_w, down_w)
    slot_ids = blocks_slots(route_ids)
    slot_rows = dispatch(normed_rows(hidden, gain_row), slot_ids).astype(jnp.float32)
    grad_rows = dispatch(grad_now.reshape(N_EXPERT, TOK_DEV, D), slot_ids).astype(jnp.float32)
    gate_act, upper = gate_up(slot_rows, gate_s, up_s)
    sigmoid_gate = jax.nn.sigmoid(gate_act)
    d_inner = jnp.einsum('enrd,eshd->esnrh', grad_rows, down_s, precision=HIGHEST)
    d_gate = round_trip(d_inner * upper * sigmoid_gate * (1.0 + gate_act * (1.0 - sigmoid_gate)))
    d_upper = round_trip(d_inner * gate_act * sigmoid_gate)
    part_rows = jnp.einsum('esnrh,esdh->esnrd', d_gate, gate_s, precision=HIGHEST)
    part_rows = round_trip(part_rows + jnp.einsum('esnrh,esdh->esnrd', d_upper, up_s, precision=HIGHEST))
    picked = collect(round_trip(lax.optimization_barrier(jnp.sum(part_rows, axis=1))), slot_ids)
    d_normed = lax.optimization_barrier(jnp.sum(mix_row.reshape(N_EXPERT, TOK_DEV, TOPK)[..., None] * picked, axis=2)).reshape(MB_TOK, D)
    _, pullback = jax.vjp(lambda values: norm_apply(values, gain_row), hidden.astype(jnp.float32))
    return (grad_now.astype(jnp.float32) + pullback(d_normed)[0]).astype(jnp.bfloat16)

def reference(tokens, norm_gain, w_gate, w_up, w_down, routes, mix_weights, cotangent):
    layers = tokens.shape[0]
    finals = [None] * layers
    input_grads = [None] * layers
    for micro_batch in range(layers):
        hidden = tokens[micro_batch]
        states = []
        for step_index in range(STEPS):
            layer_index = (micro_batch + step_index) % layers
            states.append(hidden)
            hidden = layer_forward(hidden, norm_gain[layer_index], w_gate[layer_index], w_up[layer_index], w_down[layer_index], routes[layer_index, step_index], mix_weights[layer_index, step_index])
        last_layer = (micro_batch + STEPS - 1) % layers
        finals[last_layer] = hidden
        grad_now = cotangent[last_layer]
        for step_index in reversed(range(STEPS)):
            layer_index = (micro_batch + step_index) % layers
            grad_now = layer_backward(states[step_index], grad_now, norm_gain[layer_index], w_gate[layer_index], w_up[layer_index], w_down[layer_index], routes[layer_index, step_index], mix_weights[layer_index, step_index])
        input_grads[micro_batch] = grad_now
    return (jnp.stack(finals), jnp.stack(input_grads))
```

```python
import jax
import jax.numpy as jnp
from jax import lax
from jax.experimental import pallas as pl
from jax.experimental.pallas import tpu as pltpu
from jax.sharding import PartitionSpec as P

MESH = pl.DeviceIdType.MESH
EPSILON = 1e-06
F32 = jnp.float32
BF16 = jnp.bfloat16
XS = 4
ZS = 8
NB = 16
ROWS = 8
LANES = 128


def kernel(
    tokens, gain, wgu, wdn, routes, mix, cotangent, final, grads,
    wgu_other, wd_pair, sends, recvs, back_sends, back_recvs, fold, x_all, gates, uppers, hidden1,
    hop_out, hop_in, d_own, d_other, inner,
    send_sems, recv_sems, bsend_sems, brecv_sems, w_send, w_recv, hop_send, hop_recv,
):
    width = tokens.shape[1]
    toks = tokens.shape[0]
    chunks = width // LANES
    folds = -(-chunks // 8)
    half = 64
    section = lax.axis_index("section")
    sections = lax.axis_size("section")
    me = lax.axis_index("expert")
    x = me // ZS
    z = me % ZS
    sign = 1 - 2 * (z % 2)
    own_half = z // 4
    twist = ((z + 1) // 2) % 2

    def at(xd, zd):
        return {"expert": ((xd + XS) % XS) * ZS + (zd + 2 * ZS) % ZS}

    def target(i):
        j = i % 4
        off = 2 * (j % 2) - 3 * (j // 2)
        return x + i // 4, (z + off * sign + ZS) % ZS

    def origin(i):
        j = i % 4
        off = (2 * (j % 2) - 3 * (j // 2)) * (2 * (j // 2) - 1)
        return x - i // 4, (z + off * sign + ZS) % ZS

    partner = at(x, z + sign)
    after = {"section": (section + 1) % sections}
    before = {"section": (section + sections - 1) % sections}

    barrier = pltpu.get_barrier_semaphore()

    def greet_targets(i, carry):
        xd, zd = target(i)
        pl.semaphore_signal(barrier, inc=1, device_id=at(xd, zd), device_id_type=MESH)
        return carry

    def greet_origins(i, carry):
        xd, zd = origin(i)
        pl.semaphore_signal(barrier, inc=1, device_id=at(xd, zd), device_id_type=MESH)
        return carry

    lax.fori_loop(1, NB, greet_targets, 0)
    lax.fori_loop(1, NB, greet_origins, 0)
    for neighbour in (partner, after, before):
        pl.semaphore_signal(barrier, inc=1, device_id=neighbour, device_id_type=MESH)

    def dispatch_copy(ex, i):
        xd, zd = target(i)
        block = (i // 4) * 2 + (zd // 4 + own_half) % 2
        return pltpu.make_async_remote_copy(
            src_ref=sends.at[ex, pl.ds(pl.multiple_of(block * ROWS, ROWS), ROWS), :],
            dst_ref=recvs.at[ex, pl.ds(pl.multiple_of(i * ROWS, ROWS), ROWS), :],
            send_sem=send_sems.at[ex, i],
            recv_sem=recv_sems.at[ex, i],
            device_id=at(xd, zd),
            device_id_type=MESH,
        )

    def back_copy(ex, i):
        xd, zd = origin(i)
        rows = pl.ds(pl.multiple_of(i * ROWS, ROWS), ROWS)
        return pltpu.make_async_remote_copy(
            src_ref=back_sends.at[ex, rows, :],
            dst_ref=back_recvs.at[ex, rows, :],
            send_sem=bsend_sems.at[ex, i],
            recv_sem=brecv_sems.at[ex, i],
            device_id=at(xd, zd),
            device_id_type=MESH,
        )

    def each(copy_of, ex, action):
        def body(i, carry):
            copy = copy_of(ex, i)
            if action == "start":
                copy.start()
            elif action == "recv":
                copy.wait_recv()
            else:
                copy.wait_send()
            return carry

        lax.fori_loop(1, NB, body, 0)

    def weight_copy(n):
        src, dst = (
            (wgu, wgu_other),
            (wdn.at[0:128, :], wd_pair.at[128:256, :]),
            (wdn.at[128:192, :], wd_pair.at[320:384, :]),
        )[n]
        return pltpu.make_async_remote_copy(
            src_ref=src, dst_ref=dst, send_sem=w_send.at[n], recv_sem=w_recv.at[n],
            device_id=partner, device_id_type=MESH,
        )

    def hop_copy(n):
        return pltpu.make_async_remote_copy(
            src_ref=hop_out.at[n], dst_ref=hop_in.at[n], send_sem=hop_send.at[n], recv_sem=hop_recv.at[n],
            device_id=after if n == 0 else before, device_id_type=MESH,
        )

    sub = lax.broadcasted_iota(jnp.int32, (toks, toks), 0)
    lane = lax.broadcasted_iota(jnp.int32, (toks, toks), 1)

    def column(row):
        return jnp.sum(jnp.where(sub == lane, jnp.broadcast_to(row, (toks, toks)), 0), axis=1, keepdims=True)

    def place(ids):
        dx = (ids // 2 - x + XS) % XS
        other = (ids % 2 + own_half) % 2
        return dx, other

    def plan(step):
        row_ids = routes[step : step + 1, :]
        col_ids = column(row_ids)
        same = (col_ids == row_ids).astype(jnp.int32)
        rank_col = jnp.sum(jnp.where(lane < sub, same, 0), axis=1, keepdims=True)
        rank_row = jnp.sum(jnp.where(sub < lane, same, 0), axis=0, keepdims=True)
        dx_row, other_row = place(row_ids)
        block_row = dx_row * 2 + other_row
        slot_row = jnp.where(rank_row < ROWS, block_row * ROWS + rank_row, -1)
        pick = jnp.where(sub == slot_row, 1.0, 0.0).astype(BF16)
        spill_row = jnp.where(rank_row == ROWS, block_row, -1)
        spill_sub = lax.broadcasted_iota(jnp.int32, (16, toks), 0)
        pick_spill = jnp.where(spill_sub == spill_row, 1.0, 0.0).astype(BF16)
        dx_col, other_col = place(col_ids)
        first = dx_col * 4 + other_col * (3 - 2 * twist)
        second = dx_col * 4 + jnp.where(other_col == 1, 2, 1 + 2 * twist)
        wide = lax.broadcasted_iota(jnp.int32, (toks, NB * ROWS), 1)
        plain = rank_col < ROWS
        at_first = jnp.where(plain, first * ROWS + rank_col, -1)
        at_second = jnp.where(plain, second * ROWS + rank_col, -1)
        put = jnp.where(wide == at_first, 1.0, 0.0) + jnp.where(wide == at_second, 1.0, 0.0)
        narrow = lax.broadcasted_iota(jnp.int32, (toks, NB), 1)
        spill_first = jnp.where(plain, -1, first)
        spill_second = jnp.where(plain, -1, second)
        put_spill = jnp.where(narrow == spill_first, 1.0, 0.0) + jnp.where(narrow == spill_second, 1.0, 0.0)
        weight = column(mix[step : step + 1, :])
        return pick, pick_spill, put.astype(BF16), put_spill.astype(BF16), weight

    def dot(a, b):
        return jnp.dot(a, b, preferred_element_type=F32)

    def dot_t(a, b):
        return lax.dot_general(a, b, (((1,), (1,)), ((), ())), preferred_element_type=F32)

    def fold_rows(value, count):
        for c in range(chunks):
            fold[c // 8, pl.ds(c % 8, count, stride=8), :] = value[:count, c * LANES : (c + 1) * LANES]
        for c in range(chunks, folds * 8):
            fold[c // 8, pl.ds(c % 8, count, stride=8), :] = jnp.zeros((count, LANES), F32)

    def unfold_rows(buffer):
        for b in range(folds):
            fold[b] = buffer[:, width + b * LANES : width + (b + 1) * LANES].astype(F32)
        return jnp.concatenate([fold[c // 8, pl.ds(c % 8, NB, stride=8), :] for c in range(chunks)], axis=1)

    def dispatch(ex, step_plan, values):
        pick, pick_spill, _, _, _ = step_plan
        buffer = sends.at[ex]
        buffer[:, :width] = dot(pick, values).astype(BF16)
        fold_rows(dot(pick_spill, values), 8)
        for b in range(folds):
            buffer[:, width + b * LANES : width + (b + 1) * LANES] = fold[b, 0 : 8 * ROWS, :].astype(BF16)
        each(dispatch_copy, ex, "start")
        recvs[ex, 0:ROWS, :] = sends[ex, 0:ROWS, :]

    def arrived(ex):
        each(dispatch_copy, ex, "recv")
        buffer = recvs.at[ex]
        x_all[0 : NB * ROWS, :] = buffer[:, :width]
        x_all[NB * ROWS :, :] = unfold_rows(buffer).astype(BF16)

    def send_back(ex, value_of):
        buffer = back_sends.at[ex]
        value = value_of()
        buffer[:, :width] = value[: NB * ROWS].astype(BF16)
        fold_rows(value[NB * ROWS :], NB)
        for b in range(folds):
            buffer[:, width + b * LANES : width + (b + 1) * LANES] = fold[b].astype(BF16)
        each(back_copy, ex, "start")
        back_recvs[ex, 0:ROWS, :] = back_sends[ex, 0:ROWS, :]

    def collected(ex, step_plan):
        each(back_copy, ex, "recv")
        _, _, put, put_spill, weight = step_plan
        buffer = back_recvs.at[ex]
        spill = unfold_rows(buffer).astype(BF16)
        return weight * (dot(put, buffer[:, :width]) + dot(put_spill, spill))

    low = lax.broadcasted_iota(jnp.int32, (NB * (ROWS + 1), LANES), 1) < half

    def turn(value):
        return pltpu.roll(value, half, 1)

    def project(step, wait):
        own = dot(x_all[...], wgu[...])
        if wait:
            weight_copy(0).wait_recv()
        other = dot(x_all[...], wgu_other[...])
        gates[step, :, 0:128] = own[:, 0:128]
        gates[step, :, 128:256] = other[:, 0:128]
        gates[step, :, 256:384] = jnp.where(low, own[:, 256:384], turn(other[:, 256:384]))
        uppers[step, :, 0:128] = own[:, 128:256]
        uppers[step, :, 128:256] = other[:, 128:256]
        uppers[step, :, 256:384] = jnp.where(low, turn(own[:, 256:384]), other[:, 256:384])
        gate = gates[step]
        inner[...] = (gate * jax.nn.sigmoid(gate) * uppers[step]).astype(BF16)

    def expand():
        return dot(inner[...], wd_pair[...])

    def derive(step):
        d_inner = dot_t(x_all[...], wd_pair[...])
        gate = gates[step]
        r = jax.nn.sigmoid(gate)
        d_gate = d_inner * uppers[step] * r * (1.0 + gate * (1.0 - r))
        d_upper = d_inner * gate * r
        d_own[:, 0:128] = d_gate[:, 0:128].astype(BF16)
        d_own[:, 128:256] = d_upper[:, 0:128].astype(BF16)
        d_own[:, 256:384] = jnp.where(low, d_gate[:, 256:384], turn(d_upper[:, 256:384])).astype(BF16)
        d_other[:, 0:128] = d_gate[:, 128:256].astype(BF16)
        d_other[:, 128:256] = d_upper[:, 128:256].astype(BF16)
        d_other[:, 256:384] = jnp.where(low, turn(d_gate[:, 256:384]), d_upper[:, 256:384]).astype(BF16)

    def contract():
        return dot_t(d_own[...], wgu[...]) + dot_t(d_other[...], wgu_other[...])

    def inv_scale(values):
        return lax.rsqrt(jnp.mean(values * values, axis=-1, keepdims=True) + EPSILON)

    def normed(hidden):
        values = hidden.astype(F32)
        return (values * inv_scale(values) * gain[...]).astype(BF16)

    def pulled(hidden, grad, d_normed):
        values = hidden.astype(F32)
        r = inv_scale(values)
        scaled = d_normed * gain[...]
        mean = jnp.mean(scaled * values, axis=-1, keepdims=True)
        return grad.astype(F32) + r * scaled - values * (r * r * r * mean)

    plan0 = plan(0)
    plan1 = plan(1)
    first_rows = normed(tokens[...])
    pl.semaphore_wait(barrier, 2 * (NB - 1) + 3)

    dispatch(0, plan0, first_rows)
    for n in range(3):
        weight_copy(n).start()
    wd_pair[0:128, :] = wdn[0:128, :]
    wd_pair[256:320, :] = wdn[128:192, :]
    arrived(0)
    project(0, True)
    weight_copy(1).wait_recv()
    weight_copy(2).wait_recv()
    send_back(0, expand)
    dispatch(1, plan1, cotangent[...])
    hop_out[0] = (tokens[...].astype(F32) + collected(0, plan0)).astype(BF16)
    hop_copy(0).start()
    hop_copy(0).wait_recv()
    hidden1[...] = hop_in[0]
    dispatch(2, plan1, normed(hidden1[...]))
    arrived(2)
    project(1, False)
    arrived(1)
    derive(1)
    send_back(1, contract)
    send_back(2, expand)
    grad1 = pulled(hidden1[...], cotangent[...], collected(1, plan1))
    hop_out[1] = grad1.astype(BF16)
    hop_copy(1).start()
    final[...] = (hidden1[...].astype(F32) + collected(2, plan1)).astype(BF16)
    hop_copy(1).wait_recv()
    dispatch(3, plan0, hop_in[1])
    arrived(3)
    derive(0)
    send_back(3, contract)
    grads[...] = pulled(tokens[...], hop_in[1], collected(3, plan0)).astype(BF16)

    for ex in range(4):
        each(dispatch_copy, ex, "sent")
        each(back_copy, ex, "sent")
    for n in range(3):
        weight_copy(n).wait_send()
    for n in range(2):
        hop_copy(n).wait_send()


def local(tokens, norm_gain, w_gate, w_up, w_down, routes, mix_weights, cotangent):
    toks, width = tokens.shape[1:]
    hid = w_gate.shape[3]
    gate_w, up_w = w_gate[0, 0], w_up[0, 0]
    packed = jnp.concatenate([gate_w[:, :128], up_w[:, :128], gate_w[:, 128:], up_w[:, 128:]], axis=1)
    lanes = width + 3 * LANES
    rows = NB * (ROWS + 1)
    dma = pltpu.SemaphoreType.DMA
    vmem = pl.BlockSpec(memory_space=pltpu.VMEM)
    out = jax.ShapeDtypeStruct((toks, width), BF16)
    final, grads = pl.pallas_call(
        kernel,
        out_shape=(out, out),
        in_specs=[vmem] * 7,
        out_specs=(vmem, vmem),
        scratch_shapes=[
            pltpu.VMEM((width, 2 * hid), BF16),
            pltpu.VMEM((2 * hid, width), BF16),
            pltpu.VMEM((4, 8 * ROWS, lanes), BF16),
            pltpu.VMEM((4, NB * ROWS, lanes), BF16),
            pltpu.VMEM((4, NB * ROWS, lanes), BF16),
            pltpu.VMEM((4, NB * ROWS, lanes), BF16),
            pltpu.VMEM((3, NB * ROWS, LANES), F32),
            pltpu.VMEM((rows, width), BF16),
            pltpu.VMEM((2, rows, 2 * hid), F32),
            pltpu.VMEM((2, rows, 2 * hid), F32),
            pltpu.VMEM((toks, width), BF16),
            pltpu.VMEM((2, toks, width), BF16),
            pltpu.VMEM((2, toks, width), BF16),
            pltpu.VMEM((rows, 2 * hid), BF16),
            pltpu.VMEM((rows, 2 * hid), BF16),
            pltpu.VMEM((rows, 2 * hid), BF16),
            dma((4, NB)),
            dma((4, NB)),
            dma((4, NB)),
            dma((4, NB)),
            dma((3,)),
            dma((3,)),
            dma((2,)),
            dma((2,)),
        ],
        compiler_params=pltpu.CompilerParams(
            collective_id=0, has_side_effects=True, vmem_limit_bytes=56 * 1024 * 1024
        ),
    )(
        tokens[0], norm_gain, packed, w_down[0, 0],
        routes[0, :, :, 0], mix_weights[0, :, :, 0], cotangent[0],
    )
    return final[None], grads[None]


def solution(mesh):
    in_specs = (
        P("section", "expert", None),
        P("section", None),
        P("section", "expert", None, None),
        P("section", "expert", None, None),
        P("section", "expert", None, None),
        P("section", None, "expert", None),
        P("section", None, "expert", None),
        P("section", "expert", None),
    )
    out_specs = (P("section", "expert", None), P("section", "expert", None))
    return jax.shard_map(local, mesh=mesh, in_specs=in_specs, out_specs=out_specs, check_vma=False)
```

```python
import jax
import jax.numpy as jnp
from jax import lax
from jax.experimental import pallas as pl
from jax.experimental.pallas import tpu as pltpu
from jax.sharding import PartitionSpec as P

MESH = pl.DeviceIdType.MESH
EPSILON = 1e-06
F32 = jnp.float32
BF16 = jnp.bfloat16
XS = 4
ZS = 8
NB = 16
ROWS = 8
LANES = 128
SELF = 12
FAR, NEAR = ((0, 8),), ((8, SELF), (SELF + 1, NB))
ALL = ((0, SELF), (SELF + 1, NB))
CUT = 64


def kernel(
    tokens, gain, w_gate, w_up, w_down, routes, mix, cotangent, final, grads,
    wg, wu, wd, sends, recvs, back_sends, back_recvs, fold, x_all, gates, uppers, hidden1,
    hop_out, hop_in, d_gates, d_uppers,
    send_sems, recv_sems, bsend_sems, brecv_sems, w_local, w_send, w_recv, hop_send, hop_recv,
):
    width = tokens.shape[1]
    toks = tokens.shape[0]
    hid = w_gate.shape[0]
    chunks = width // LANES
    folds = -(-chunks // 8)
    section = lax.axis_index("section")
    sections = lax.axis_size("section")
    me = lax.axis_index("expert")
    x = me // ZS
    z = me % ZS
    sign = 1 - 2 * (z % 2)
    own_half = z // 4
    twist = ((z + 1) // 2) % 2

    def at(xd, zd):
        return {"expert": ((xd + XS) % XS) * ZS + (zd + 2 * ZS) % ZS}

    def target(i):
        j = i // 4
        off = (j - 3) * (1 - 2 * (j % 2))
        return x + i % 4, (z + off * sign + ZS) % ZS

    def origin(i):
        return x - i % 4, (z + (i // 4 - 3) * sign + ZS) % ZS

    partner = at(x, z + sign)
    after = {"section": (section + 1) % sections}
    before = {"section": (section + sections - 1) % sections}

    def weight_local(n):
        src, dst = ((w_gate, wg), (w_up, wu), (w_down, wd))[n]
        return pltpu.make_async_copy(src, dst.at[0:hid, :], w_local.at[n])

    def weight_copy(n):
        src, dst = ((w_gate, wg), (w_up, wu), (w_down, wd))[n]
        return pltpu.make_async_remote_copy(
            src_ref=src, dst_ref=dst.at[hid : 2 * hid, :], send_sem=w_send.at[n], recv_sem=w_recv.at[n],
            device_id=partner, device_id_type=MESH,
        )

    def hop_copy(n):
        return pltpu.make_async_remote_copy(
            src_ref=hop_out.at[n], dst_ref=hop_in.at[n], send_sem=hop_send.at[n], recv_sem=hop_recv.at[n],
            device_id=after if n == 0 else before, device_id_type=MESH,
        )

    def over(ranges, action):
        def body(i, carry):
            action(i)
            return carry

        for low, high in ranges:
            lax.fori_loop(low, high, body, 0)

    barrier = pltpu.get_barrier_semaphore()

    def greet(place_of):
        def action(i):
            xd, zd = place_of(i)
            pl.semaphore_signal(barrier, inc=1, device_id=at(xd, zd), device_id_type=MESH)

        over(ALL, action)

    greet(target)
    greet(origin)
    for neighbour in (partner, after, before):
        pl.semaphore_signal(barrier, inc=1, device_id=neighbour, device_id_type=MESH)
    for n in range(3):
        weight_local(n).start()

    def dispatch_copy(ex, i):
        xd, zd = target(i)
        block = (i % 4) * 2 + (zd // 4 + own_half) % 2
        return pltpu.make_async_remote_copy(
            src_ref=sends.at[ex, pl.ds(pl.multiple_of(block * ROWS, ROWS), ROWS), :],
            dst_ref=recvs.at[ex, pl.ds(pl.multiple_of(i * ROWS, ROWS), ROWS), :],
            send_sem=send_sems.at[ex, i],
            recv_sem=recv_sems.at[ex, i],
            device_id=at(xd, zd),
            device_id_type=MESH,
        )

    def back_copy(ex, i):
        xd, zd = origin(i)
        rows = pl.ds(pl.multiple_of(i * ROWS, ROWS), ROWS)
        return pltpu.make_async_remote_copy(
            src_ref=back_sends.at[ex, rows, :],
            dst_ref=back_recvs.at[ex, rows, :],
            send_sem=bsend_sems.at[ex, i],
            recv_sem=brecv_sems.at[ex, i],
            device_id=at(xd, zd),
            device_id_type=MESH,
        )

    def each(copy_of, ex, action, ranges):
        def one(i):
            copy = copy_of(ex, i)
            if action == "start":
                copy.start()
            elif action == "recv":
                copy.wait_recv()
            else:
                copy.wait_send()

        over(ranges, one)

    sub = lax.broadcasted_iota(jnp.int32, (toks, toks), 0)
    lane = lax.broadcasted_iota(jnp.int32, (toks, toks), 1)

    def column(row):
        return jnp.sum(jnp.where(sub == lane, jnp.broadcast_to(row, (toks, toks)), 0), axis=1, keepdims=True)

    def place(ids):
        dx = (ids // 2 - x + XS) % XS
        other = (ids % 2 + own_half) % 2
        return dx, other

    def plan(step):
        row_ids = routes[step : step + 1, :]
        col_ids = column(row_ids)
        same = (col_ids == row_ids).astype(jnp.int32)
        rank_col = jnp.sum(jnp.where(lane < sub, same, 0), axis=1, keepdims=True)
        rank_row = jnp.sum(jnp.where(sub < lane, same, 0), axis=0, keepdims=True)
        dx_row, other_row = place(row_ids)
        block_row = dx_row * 2 + other_row
        slot_row = jnp.where(rank_row < ROWS, block_row * ROWS + rank_row, -1)
        pick = jnp.where(sub == slot_row, 1.0, 0.0).astype(BF16)
        spill_row = jnp.where(rank_row == ROWS, block_row, -1)
        spill_sub = lax.broadcasted_iota(jnp.int32, (16, toks), 0)
        pick_spill = jnp.where(spill_sub == spill_row, 1.0, 0.0).astype(BF16)
        dx_col, other_col = place(col_ids)
        first = jnp.where(other_col == 1, 0, 12) + dx_col
        second = jnp.where(other_col == 1, 2 - twist, 1 + twist) * 4 + dx_col
        wide = lax.broadcasted_iota(jnp.int32, (toks, NB * ROWS), 1)
        plain = rank_col < ROWS
        at_first = jnp.where(plain, first * ROWS + rank_col, -1)
        at_second = jnp.where(plain, second * ROWS + rank_col, -1)
        put = jnp.where(wide == at_first, 1.0, 0.0) + jnp.where(wide == at_second, 1.0, 0.0)
        narrow = lax.broadcasted_iota(jnp.int32, (toks, NB), 1)
        spill_first = jnp.where(plain, -1, first)
        spill_second = jnp.where(plain, -1, second)
        put_spill = jnp.where(narrow == spill_first, 1.0, 0.0) + jnp.where(narrow == spill_second, 1.0, 0.0)
        weight = column(mix[step : step + 1, :])
        return pick, pick_spill, put.astype(BF16), put_spill.astype(BF16), weight

    def dot(a, b):
        return jnp.dot(a, b, preferred_element_type=F32)

    def dot_t(a, b):
        return lax.dot_general(a, b, (((1,), (1,)), ((), ())), preferred_element_type=F32)

    def fold_rows(value, count, buffer, rows):
        for c in range(chunks):
            fold[c // 8, pl.ds(c % 8, count, stride=8), :] = value[:count, c * LANES : (c + 1) * LANES]
        for c in range(chunks, folds * 8):
            fold[c // 8, pl.ds(c % 8, count, stride=8), :] = jnp.zeros((count, LANES), F32)
        for b in range(folds):
            buffer[0:rows, width + b * LANES : width + (b + 1) * LANES] = fold[b, 0:rows, :].astype(BF16)

    def unfold_rows(buffer):
        for b in range(folds):
            fold[b] = buffer[:, width + b * LANES : width + (b + 1) * LANES].astype(F32)
        return jnp.concatenate([fold[c // 8, pl.ds(c % 8, NB, stride=8), :] for c in range(chunks)], axis=1)

    def pack(ex, step_plan, values):
        pick, pick_spill, _, _, _ = step_plan
        buffer = sends.at[ex]
        buffer[:, :width] = dot(pick, values).astype(BF16)
        fold_rows(dot(pick_spill, values), 8, buffer, 8 * ROWS)
        recvs[ex, SELF * ROWS : (SELF + 1) * ROWS, :] = sends[ex, 0:ROWS, :]

    def arrived(ex):
        each(dispatch_copy, ex, "recv", ALL)
        buffer = recvs.at[ex]
        x_all[0:CUT, :] = buffer[0:CUT, :width]
        x_all[CUT : CUT + NB, :] = unfold_rows(buffer).astype(BF16)
        x_all[CUT + NB :, :] = buffer[CUT:, :width]

    def send_back(ex, value_of, start):
        buffer = back_sends.at[ex]
        value = value_of(slice(0, CUT + NB))
        buffer[0:CUT, :width] = value[:CUT].astype(BF16)
        fold_rows(value[CUT:], NB, buffer, NB * ROWS)
        if start:
            each(back_copy, ex, "start", FAR)
        buffer[CUT:, :width] = value_of(slice(CUT + NB, NB * (ROWS + 1))).astype(BF16)
        if start:
            each(back_copy, ex, "start", NEAR)
        back_recvs[ex, SELF * ROWS : (SELF + 1) * ROWS, :] = back_sends[ex, SELF * ROWS : (SELF + 1) * ROWS, :]

    def collected(ex, step_plan):
        each(back_copy, ex, "recv", ALL)
        _, _, put, put_spill, weight = step_plan
        buffer = back_recvs.at[ex]
        spill = unfold_rows(buffer).astype(BF16)
        return weight * (dot(put, buffer[:, :width]) + dot(put_spill, spill))

    def activate(step):
        gate = gates[step]
        d_gates[...] = (gate * jax.nn.sigmoid(gate) * uppers[step]).astype(BF16)

    def expand(rows):
        return dot(d_gates[rows, :], wd[...])

    def derive(step):
        d_inner = dot_t(x_all[...], wd[...])
        gate = gates[step]
        r = jax.nn.sigmoid(gate)
        d_gates[...] = (d_inner * uppers[step] * r * (1.0 + gate * (1.0 - r))).astype(BF16)
        d_uppers[...] = (d_inner * gate * r).astype(BF16)

    def contract(rows):
        return dot(d_gates[rows, :], wg[...]) + dot(d_uppers[rows, :], wu[...])

    def inv_scale(values):
        return lax.rsqrt(jnp.mean(values * values, axis=-1, keepdims=True) + EPSILON)

    def normed(hidden):
        values = hidden.astype(F32)
        return (values * inv_scale(values) * gain[...]).astype(BF16)

    def pulled(hidden, grad, d_normed):
        values = hidden.astype(F32)
        r = inv_scale(values)
        scaled = d_normed * gain[...]
        mean = jnp.mean(scaled * values, axis=-1, keepdims=True)
        return grad.astype(F32) + r * scaled - values * (r * r * r * mean)

    plan0 = plan(0)
    pack(0, plan0, normed(tokens[...]))
    pl.semaphore_wait(barrier, 2 * (NB - 1) + 3)
    weight_copy(0).start()
    weight_copy(1).start()
    each(dispatch_copy, 0, "start", ALL)
    plan1 = plan(1)
    pack(1, plan1, cotangent[...])
    each(dispatch_copy, 1, "start", NEAR)
    for n in range(3):
        weight_local(n).wait()
    arrived(0)
    weight_copy(2).start()
    weight_copy(0).wait_recv()
    gates[0] = dot_t(x_all[...], wg[...])
    weight_copy(1).wait_recv()
    uppers[0] = dot_t(x_all[...], wu[...])
    activate(0)
    weight_copy(2).wait_recv()
    send_back(0, expand, True)
    hop_out[0] = (tokens[...].astype(F32) + collected(0, plan0)).astype(BF16)
    hop_copy(0).start()
    each(dispatch_copy, 1, "start", FAR)
    hop_copy(0).wait_recv()
    hidden1[...] = hop_in[0]
    pack(2, plan1, normed(hidden1[...]))
    each(dispatch_copy, 2, "start", ALL)
    arrived(2)
    gates[1] = dot_t(x_all[...], wg[...])
    uppers[1] = dot_t(x_all[...], wu[...])
    arrived(1)
    derive(1)
    send_back(1, contract, True)
    activate(1)
    send_back(2, expand, False)
    grad1 = pulled(hidden1[...], cotangent[...], collected(1, plan1))
    hop_out[1] = grad1.astype(BF16)
    hop_copy(1).start()
    each(back_copy, 2, "start", ALL)
    hop_copy(1).wait_recv()
    pack(3, plan0, hop_in[1])
    each(dispatch_copy, 3, "start", ALL)
    final[...] = (hidden1[...].astype(F32) + collected(2, plan1)).astype(BF16)
    arrived(3)
    derive(0)
    send_back(3, contract, True)
    grads[...] = pulled(tokens[...], hop_in[1], collected(3, plan0)).astype(BF16)

    for ex in range(4):
        each(dispatch_copy, ex, "sent", ALL)
        each(back_copy, ex, "sent", ALL)
    for n in range(3):
        weight_copy(n).wait_send()
    for n in range(2):
        hop_copy(n).wait_send()


def local(tokens, norm_gain, w_gate, w_up, w_down, routes, mix_weights, cotangent):
    toks, width = tokens.shape[1:]
    hid = w_gate.shape[3]
    lanes = width + 3 * LANES
    rows = NB * (ROWS + 1)
    dma = pltpu.SemaphoreType.DMA
    vmem = pl.BlockSpec(memory_space=pltpu.VMEM)
    anywhere = pl.BlockSpec(memory_space=pl.ANY)
    out = jax.ShapeDtypeStruct((toks, width), BF16)
    final, grads = pl.pallas_call(
        kernel,
        out_shape=(out, out),
        in_specs=[vmem] * 2 + [anywhere] * 3 + [vmem] * 3,
        out_specs=(vmem, vmem),
        scratch_shapes=[
            pltpu.VMEM((2 * hid, width), BF16),
            pltpu.VMEM((2 * hid, width), BF16),
            pltpu.VMEM((2 * hid, width), BF16),
            pltpu.VMEM((4, 8 * ROWS, lanes), BF16),
            pltpu.VMEM((4, NB * ROWS, lanes), BF16),
            pltpu.VMEM((4, NB * ROWS, lanes), BF16),
            pltpu.VMEM((4, NB * ROWS, lanes), BF16),
            pltpu.VMEM((3, NB * ROWS, LANES), F32),
            pltpu.VMEM((rows, width), BF16),
            pltpu.VMEM((2, rows, 2 * hid), F32),
            pltpu.VMEM((2, rows, 2 * hid), F32),
            pltpu.VMEM((toks, width), BF16),
            pltpu.VMEM((2, toks, width), BF16),
            pltpu.VMEM((2, toks, width), BF16),
            pltpu.VMEM((rows, 2 * hid), BF16),
            pltpu.VMEM((rows, 2 * hid), BF16),
            dma((4, NB)),
            dma((4, NB)),
            dma((4, NB)),
            dma((4, NB)),
            dma((3,)),
            dma((3,)),
            dma((3,)),
            dma((2,)),
            dma((2,)),
        ],
        compiler_params=pltpu.CompilerParams(
            collective_id=0, has_side_effects=True, vmem_limit_bytes=56 * 1024 * 1024
        ),
    )(
        tokens[0], norm_gain, w_gate[0, 0].T, w_up[0, 0].T, w_down[0, 0],
        routes[0, :, :, 0], mix_weights[0, :, :, 0], cotangent[0],
    )
    return final[None], grads[None]


def solution(mesh):
    in_specs = (
        P("section", "expert", None),
        P("section", None),
        P("section", "expert", None, None),
        P("section", "expert", None, None),
        P("section", "expert", None, None),
        P("section", None, "expert", None),
        P("section", None, "expert", None),
        P("section", "expert", None),
    )
    out_specs = (P("section", "expert", None), P("section", "expert", None))
    return jax.shard_map(local, mesh=mesh, in_specs=in_specs, out_specs=out_specs, check_vma=False)
```

```python
import jax
import jax.numpy as jnp
from jax import lax
from jax.experimental import pallas as pl
from jax.experimental.pallas import tpu as pltpu
from jax.sharding import PartitionSpec as P

MESH = pl.DeviceIdType.MESH
EPSILON = 1e-06
F32 = jnp.float32
BF16 = jnp.bfloat16
XS = 4
ZS = 8
NB = 16
ROWS = 8
LANES = 128
SELF = 12
FAR, NEAR = ((0, 8),), ((8, SELF), (SELF + 1, NB))
ALL = ((0, SELF), (SELF + 1, NB))
PARTS = (FAR, NEAR)
HALF = 8


def kernel(
    tokens, gain, w_gate, w_up, w_down, routes, mix, cotangent, final, grads,
    wg, wu, wd, sends, recvs, back_sends, back_recvs, fold, x_all, gates, uppers, hidden1,
    hop_out, hop_in,
    send_sems, recv_sems, bsend_sems, brecv_sems, w_send, w_recv, hop_send, hop_recv,
):
    width = tokens.shape[1]
    toks = tokens.shape[0]
    hid = w_gate.shape[0]
    chunks = width // LANES
    folds = -(-chunks // 8)
    section = lax.axis_index("section")
    sections = lax.axis_size("section")
    me = lax.axis_index("expert")
    x = me // ZS
    z = me % ZS
    sign = 1 - 2 * (z % 2)
    own_half = z // 4
    twist = ((z + 1) // 2) % 2

    def at(xd, zd):
        return {"expert": ((xd + XS) % XS) * ZS + (zd + 2 * ZS) % ZS}

    def target(i):
        j = i // 4
        off = (j - 3) * (1 - 2 * (j % 2))
        return x + i % 4, (z + off * sign + ZS) % ZS

    def origin(i):
        return x - i % 4, (z + (i // 4 - 3) * sign + ZS) % ZS

    partner = at(x, z + sign)
    after = {"section": (section + 1) % sections}
    before = {"section": (section + sections - 1) % sections}

    def weight_copy(n):
        src, dst = ((w_gate, wg), (w_up, wu), (w_down, wd))[n]
        return pltpu.make_async_remote_copy(
            src_ref=src, dst_ref=dst.at[hid : 2 * hid, :], send_sem=w_send.at[n], recv_sem=w_recv.at[n],
            device_id=partner, device_id_type=MESH,
        )

    def hop_copy(n):
        return pltpu.make_async_remote_copy(
            src_ref=hop_out.at[n], dst_ref=hop_in.at[n], send_sem=hop_send.at[n], recv_sem=hop_recv.at[n],
            device_id=after if n == 0 else before, device_id_type=MESH,
        )

    def over(ranges, action):
        def body(i, carry):
            action(i)
            return carry

        for low, high in ranges:
            lax.fori_loop(low, high, body, 0)

    barrier = pltpu.get_barrier_semaphore()

    def greet(place_of):
        def action(i):
            xd, zd = place_of(i)
            pl.semaphore_signal(barrier, inc=1, device_id=at(xd, zd), device_id_type=MESH)

        over(ALL, action)

    greet(target)
    greet(origin)
    for neighbour in (partner, after, before):
        pl.semaphore_signal(barrier, inc=1, device_id=neighbour, device_id_type=MESH)

    def dispatch_copy(ex, i):
        xd, zd = target(i)
        block = (i % 4) * 2 + (zd // 4 + own_half) % 2
        return pltpu.make_async_remote_copy(
            src_ref=sends.at[ex, pl.ds(pl.multiple_of(block * ROWS, ROWS), ROWS), :],
            dst_ref=recvs.at[ex, pl.ds(pl.multiple_of(i * ROWS, ROWS), ROWS), :],
            send_sem=send_sems.at[ex, i],
            recv_sem=recv_sems.at[ex, i],
            device_id=at(xd, zd),
            device_id_type=MESH,
        )

    def back_copy(ex, i):
        xd, zd = origin(i)
        rows = pl.ds(pl.multiple_of(i * ROWS, ROWS), ROWS)
        return pltpu.make_async_remote_copy(
            src_ref=back_sends.at[ex, rows, :],
            dst_ref=back_recvs.at[ex, rows, :],
            send_sem=bsend_sems.at[ex, i],
            recv_sem=brecv_sems.at[ex, i],
            device_id=at(xd, zd),
            device_id_type=MESH,
        )

    def each(copy_of, ex, action, ranges):
        def one(i):
            copy = copy_of(ex, i)
            if action == "start":
                copy.start()
            elif action == "recv":
                copy.wait_recv()
            else:
                copy.wait_send()

        over(ranges, one)

    sub = lax.broadcasted_iota(jnp.int32, (toks, toks), 0)
    lane = lax.broadcasted_iota(jnp.int32, (toks, toks), 1)

    def column(row):
        return jnp.sum(jnp.where(sub == lane, jnp.broadcast_to(row, (toks, toks)), 0), axis=1, keepdims=True)

    def place(ids):
        dx = (ids // 2 - x + XS) % XS
        other = (ids % 2 + own_half) % 2
        return dx, other

    def plan(step):
        row_ids = routes[step : step + 1, :]
        col_ids = column(row_ids)
        same = (col_ids == row_ids).astype(jnp.int32)
        rank_col = jnp.sum(jnp.where(lane < sub, same, 0), axis=1, keepdims=True)
        rank_row = jnp.sum(jnp.where(sub < lane, same, 0), axis=0, keepdims=True)
        dx_row, other_row = place(row_ids)
        block_row = dx_row * 2 + other_row
        slot_row = jnp.where(rank_row < ROWS, block_row * ROWS + rank_row, -1)
        pick = jnp.where(sub == slot_row, 1.0, 0.0).astype(BF16)
        spill_row = jnp.where(rank_row == ROWS, block_row, -1)
        spill_sub = lax.broadcasted_iota(jnp.int32, (16, toks), 0)
        pick_spill = jnp.where(spill_sub == spill_row, 1.0, 0.0).astype(BF16)
        dx_col, other_col = place(col_ids)
        first = jnp.where(other_col == 1, 0, 12) + dx_col
        second = jnp.where(other_col == 1, 2 - twist, 1 + twist) * 4 + dx_col
        plain = rank_col < ROWS
        wide = lax.broadcasted_iota(jnp.int32, (toks, HALF * ROWS), 1)
        narrow = lax.broadcasted_iota(jnp.int32, (toks, HALF), 1)
        puts, put_spills = [], []
        for part in range(2):
            begin = part * HALF
            put, put_spill = 0.0, 0.0
            for block in (first, second):
                inside = (block >= begin) & (block < begin + HALF)
                slot = jnp.where(plain & inside, (block - begin) * ROWS + rank_col, -1)
                put = put + jnp.where(wide == slot, 1.0, 0.0)
                slot = jnp.where(plain, -1, block - begin)
                put_spill = put_spill + jnp.where(narrow == slot, 1.0, 0.0)
            puts.append(put.astype(BF16))
            put_spills.append(put_spill.astype(BF16))
        weight = column(mix[step : step + 1, :])
        return pick, pick_spill, puts, put_spills, weight

    def dot(a, b):
        return jnp.dot(a, b, preferred_element_type=F32)

    def dot_t(a, b):
        return lax.dot_general(a, b, (((1,), (1,)), ((), ())), preferred_element_type=F32)

    def fold_rows(value, buffer):
        for c in range(chunks):
            fold[c // 8, pl.ds(c % 8, 8, stride=8), :] = value[:8, c * LANES : (c + 1) * LANES]
        for c in range(chunks, folds * 8):
            fold[c // 8, pl.ds(c % 8, 8, stride=8), :] = jnp.zeros((8, LANES), F32)
        for b in range(folds):
            buffer[:, width + b * LANES : width + (b + 1) * LANES] = fold[b].astype(BF16)

    def unfold_rows(buffer):
        for b in range(folds):
            fold[b] = buffer[:, width + b * LANES : width + (b + 1) * LANES].astype(F32)
        return jnp.concatenate([fold[c // 8, pl.ds(c % 8, 8, stride=8), :] for c in range(chunks)], axis=1)

    def pack(ex, step_plan, values):
        pick, pick_spill, _, _, _ = step_plan
        buffer = sends.at[ex]
        buffer[:, :width] = dot(pick, values).astype(BF16)
        fold_rows(dot(pick_spill, values), buffer)
        recvs[ex, SELF * ROWS : (SELF + 1) * ROWS, :] = sends[ex, 0:ROWS, :]

    def part_rows(part):
        return slice(part * HALF * ROWS, (part + 1) * HALF * ROWS)

    def arrived(ex, part):
        each(dispatch_copy, ex, "recv", PARTS[part])
        buffer = recvs.at[ex, part_rows(part), :]
        x_all[part, 0 : HALF * ROWS, :] = buffer[:, :width]
        x_all[part, HALF * ROWS : HALF * ROWS + 8, :] = unfold_rows(buffer).astype(BF16)

    def send_back(ex, part, value, start):
        buffer = back_sends.at[ex, part_rows(part), :]
        buffer[:, :width] = value[: HALF * ROWS].astype(BF16)
        fold_rows(value[HALF * ROWS :], buffer)
        if start:
            each(back_copy, ex, "start", PARTS[part])
        if part == 1:
            back_recvs[ex, SELF * ROWS : (SELF + 1) * ROWS, :] = back_sends[ex, SELF * ROWS : (SELF + 1) * ROWS, :]

    def collected(ex, step_plan):
        _, _, puts, put_spills, weight = step_plan
        total = None
        for part in (1, 0):
            each(back_copy, ex, "recv", PARTS[part])
            buffer = back_recvs.at[ex, part_rows(part), :]
            spill = unfold_rows(buffer).astype(BF16)
            term = dot(puts[part], buffer[:, :width]) + dot(put_spills[part], spill)
            total = term if total is None else total + term
        return weight * total

    def project(step, part):
        gates[step, part] = dot_t(x_all[part], wg[...])
        uppers[step, part] = dot_t(x_all[part], wu[...])

    def expand(step, part):
        gate = gates[step, part]
        return dot((gate * jax.nn.sigmoid(gate) * uppers[step, part]).astype(BF16), wd[...])

    def derive(step, part):
        d_inner = dot_t(x_all[part], wd[...])
        gate = gates[step, part]
        r = jax.nn.sigmoid(gate)
        d_gate = (d_inner * uppers[step, part] * r * (1.0 + gate * (1.0 - r))).astype(BF16)
        d_upper = (d_inner * gate * r).astype(BF16)
        return dot(d_gate, wg[...]) + dot(d_upper, wu[...])

    def inv_scale(values):
        return lax.rsqrt(jnp.mean(values * values, axis=-1, keepdims=True) + EPSILON)

    def normed(hidden):
        values = hidden.astype(F32)
        return (values * inv_scale(values) * gain[...]).astype(BF16)

    def pulled(hidden, grad, d_normed):
        values = hidden.astype(F32)
        r = inv_scale(values)
        scaled = d_normed * gain[...]
        mean = jnp.mean(scaled * values, axis=-1, keepdims=True)
        return grad.astype(F32) + r * scaled - values * (r * r * r * mean)

    plan0 = plan(0)
    pack(0, plan0, normed(tokens[...]))
    pl.semaphore_wait(barrier, 2 * (NB - 1) + 3)
    weight_copy(0).start()
    weight_copy(1).start()
    each(dispatch_copy, 0, "start", ALL)
    plan1 = plan(1)
    pack(1, plan1, cotangent[...])
    each(dispatch_copy, 1, "start", NEAR)
    for own, pair in ((w_gate, wg), (w_up, wu), (w_down, wd)):
        pair[0:hid, :] = own[...]
    x_all[:, HALF * ROWS + 8 :, :] = jnp.zeros((2, 8, width), BF16)
    arrived(0, 1)
    arrived(0, 0)
    weight_copy(2).start()
    weight_copy(0).wait_recv()
    weight_copy(1).wait_recv()
    project(0, 0)
    project(0, 1)
    weight_copy(2).wait_recv()
    send_back(0, 0, expand(0, 0), True)
    send_back(0, 1, expand(0, 1), True)
    hop_out[0] = (tokens[...].astype(F32) + collected(0, plan0)).astype(BF16)
    hop_copy(0).start()
    each(dispatch_copy, 1, "start", FAR)
    hop_copy(0).wait_recv()
    hidden1[...] = hop_in[0]
    pack(2, plan1, normed(hidden1[...]))
    each(dispatch_copy, 2, "start", ALL)
    for part in (1, 0):
        arrived(2, part)
        project(1, part)
        arrived(1, part)
        send_back(1, part, derive(1, part), True)
    send_back(2, 1, expand(1, 1), False)
    send_back(2, 0, expand(1, 0), False)
    grad1 = pulled(hidden1[...], cotangent[...], collected(1, plan1))
    hop_out[1] = grad1.astype(BF16)
    hop_copy(1).start()
    each(back_copy, 2, "start", NEAR)
    each(back_copy, 2, "start", ((4, 8),))
    hop_copy(1).wait_recv()
    pack(3, plan0, hop_in[1])
    each(dispatch_copy, 3, "start", ALL)
    arrived(3, 1)
    send_back(3, 1, derive(0, 1), True)
    arrived(3, 0)
    each(back_copy, 2, "start", ((0, 4),))
    send_back(3, 0, derive(0, 0), True)
    final[...] = (hidden1[...].astype(F32) + collected(2, plan1)).astype(BF16)
    grads[...] = pulled(tokens[...], hop_in[1], collected(3, plan0)).astype(BF16)

    for ex in range(4):
        each(dispatch_copy, ex, "sent", ALL)
        each(back_copy, ex, "sent", ALL)
    for n in range(3):
        weight_copy(n).wait_send()
    for n in range(2):
        hop_copy(n).wait_send()


def local(tokens, norm_gain, w_gate, w_up, w_down, routes, mix_weights, cotangent):
    toks, width = tokens.shape[1:]
    hid = w_gate.shape[3]
    lanes = width + 3 * LANES
    rows = HALF * (ROWS + 2)
    dma = pltpu.SemaphoreType.DMA
    vmem = pl.BlockSpec(memory_space=pltpu.VMEM)
    out = jax.ShapeDtypeStruct((toks, width), BF16)
    final, grads = pl.pallas_call(
        kernel,
        out_shape=(out, out),
        in_specs=[vmem] * 8,
        out_specs=(vmem, vmem),
        scratch_shapes=[
            pltpu.VMEM((2 * hid, width), BF16),
            pltpu.VMEM((2 * hid, width), BF16),
            pltpu.VMEM((2 * hid, width), BF16),
            pltpu.VMEM((4, 8 * ROWS, lanes), BF16),
            pltpu.VMEM((4, NB * ROWS, lanes), BF16),
            pltpu.VMEM((4, NB * ROWS, lanes), BF16),
            pltpu.VMEM((4, NB * ROWS, lanes), BF16),
            pltpu.VMEM((3, HALF * ROWS, LANES), F32),
            pltpu.VMEM((2, rows, width), BF16),
            pltpu.VMEM((2, 2, rows, 2 * hid), F32),
            pltpu.VMEM((2, 2, rows, 2 * hid), F32),
            pltpu.VMEM((toks, width), BF16),
            pltpu.VMEM((2, toks, width), BF16),
            pltpu.VMEM((2, toks, width), BF16),
            dma((4, NB)),
            dma((4, NB)),
            dma((4, NB)),
            dma((4, NB)),
            dma((3,)),
            dma((3,)),
            dma((2,)),
            dma((2,)),
        ],
        compiler_params=pltpu.CompilerParams(
            collective_id=0, has_side_effects=True, vmem_limit_bytes=56 * 1024 * 1024
        ),
    )(
        tokens[0], norm_gain, w_gate[0, 0].T, w_up[0, 0].T, w_down[0, 0],
        routes[0, :, :, 0], mix_weights[0, :, :, 0], cotangent[0],
    )
    return final[None], grads[None]


def solution(mesh):
    in_specs = (
        P("section", "expert", None),
        P("section", None),
        P("section", "expert", None, None),
        P("section", "expert", None, None),
        P("section", "expert", None, None),
        P("section", None, "expert", None),
        P("section", None, "expert", None),
        P("section", "expert", None),
    )
    out_specs = (P("section", "expert", None), P("section", "expert", None))
    return jax.shard_map(local, mesh=mesh, in_specs=in_specs, out_specs=out_specs, check_vma=False)
```

```python
import jax
import jax.numpy as jnp
from jax import lax
from jax.experimental import pallas as pl
from jax.experimental.pallas import tpu as pltpu
from jax.sharding import PartitionSpec as P

MESH = pl.DeviceIdType.MESH
EPSILON = 1e-06
F32 = jnp.float32
BF16 = jnp.bfloat16
XS = 4
ZS = 8
NB = 16
ROWS = 8
LANES = 128
SELF = 12
FAR, NEAR = ((0, 8),), ((8, SELF), (SELF + 1, NB))
ALL = ((0, SELF), (SELF + 1, NB))
PARTS = (FAR, NEAR)
LAST, MIDDLE = ((0, 4),), ((4, 8),)
HALF = 8


def kernel(
    tokens, gain, w_gate, w_up, w_down, routes, mix, cotangent, final, grads,
    wg, wu, wd, sends, recvs, back_sends, back_recvs, fold, x_all, gates, uppers, hidden1,
    hop_out, hop_in,
    send_sems, recv_sems, bsend_sems, brecv_sems, w_local, w_send, w_recv, hop_send, hop_recv,
):
    width = tokens.shape[1]
    toks = tokens.shape[0]
    hid = w_gate.shape[0]
    chunks = width // LANES
    folds = -(-chunks // 8)
    section = lax.axis_index("section")
    sections = lax.axis_size("section")
    me = lax.axis_index("expert")
    x = me // ZS
    z = me % ZS
    sign = 1 - 2 * (z % 2)
    own_half = z // 4
    twist = ((z + 1) // 2) % 2

    def at(xd, zd):
        return {"expert": ((xd + XS) % XS) * ZS + (zd + 2 * ZS) % ZS}

    def target(i):
        j = i // 4
        off = (j - 3) * (1 - 2 * (j % 2))
        return x + i % 4, (z + off * sign + ZS) % ZS

    def origin(i):
        return x - i % 4, (z + (i // 4 - 3) * sign + ZS) % ZS

    partner = at(x, z + sign)
    after = {"section": (section + 1) % sections}
    before = {"section": (section + sections - 1) % sections}

    def weight_local(n):
        src, dst = ((w_gate, wg), (w_up, wu), (w_down, wd))[n]
        return pltpu.make_async_copy(src, dst.at[0:hid, :], w_local.at[n])

    def weight_copy(n):
        src, dst = ((w_gate, wg), (w_up, wu), (w_down, wd))[n]
        return pltpu.make_async_remote_copy(
            src_ref=src, dst_ref=dst.at[hid : 2 * hid, :], send_sem=w_send.at[n], recv_sem=w_recv.at[n],
            device_id=partner, device_id_type=MESH,
        )

    def hop_copy(n):
        return pltpu.make_async_remote_copy(
            src_ref=hop_out.at[n], dst_ref=hop_in.at[n], send_sem=hop_send.at[n], recv_sem=hop_recv.at[n],
            device_id=after if n == 0 else before, device_id_type=MESH,
        )

    def over(ranges, action):
        def body(i, carry):
            action(i)
            return carry

        for low, high in ranges:
            lax.fori_loop(low, high, body, 0)

    barrier = pltpu.get_barrier_semaphore()

    def greet(i):
        j = i // 4
        zd = z + (j - 3 + j // 4) * sign
        pl.semaphore_signal(barrier, inc=1, device_id=at(x + i % 4, zd), device_id_type=MESH)

    over(((0, SELF), (SELF + 1, NB + 4)), greet)
    for neighbour in (partner, after, before):
        pl.semaphore_signal(barrier, inc=1, device_id=neighbour, device_id_type=MESH)

    def dispatch_copy(ex, i):
        xd, zd = target(i)
        block = (i % 4) * 2 + (zd // 4 + own_half) % 2
        return pltpu.make_async_remote_copy(
            src_ref=sends.at[ex, pl.ds(pl.multiple_of(block * ROWS, ROWS), ROWS), :],
            dst_ref=recvs.at[ex, pl.ds(pl.multiple_of(i * ROWS, ROWS), ROWS), :],
            send_sem=send_sems.at[ex, i],
            recv_sem=recv_sems.at[ex, i],
            device_id=at(xd, zd),
            device_id_type=MESH,
        )

    def back_copy(ex, i):
        xd, zd = origin(i)
        rows = pl.ds(pl.multiple_of(i * ROWS, ROWS), ROWS)
        return pltpu.make_async_remote_copy(
            src_ref=back_sends.at[ex, rows, :],
            dst_ref=back_recvs.at[ex, rows, :],
            send_sem=bsend_sems.at[ex, i],
            recv_sem=brecv_sems.at[ex, i],
            device_id=at(xd, zd),
            device_id_type=MESH,
        )

    def each(copy_of, ex, action, ranges):
        def one(i):
            copy = copy_of(ex, i)
            if action == "start":
                copy.start()
            elif action == "recv":
                copy.wait_recv()
            else:
                copy.wait_send()

        over(ranges, one)

    sub = lax.broadcasted_iota(jnp.int32, (toks, toks), 0)
    lane = lax.broadcasted_iota(jnp.int32, (toks, toks), 1)

    def column(row):
        return jnp.sum(jnp.where(sub == lane, jnp.broadcast_to(row, (toks, toks)), 0), axis=1, keepdims=True)

    def place(ids):
        dx = (ids // 2 - x + XS) % XS
        other = (ids % 2 + own_half) % 2
        return dx, other

    def plan(step):
        row_ids = routes[step : step + 1, :]
        col_ids = column(row_ids)
        same = (col_ids == row_ids).astype(jnp.int32)
        rank_col = jnp.sum(jnp.where(lane < sub, same, 0), axis=1, keepdims=True)
        rank_row = jnp.sum(jnp.where(sub < lane, same, 0), axis=0, keepdims=True)
        dx_row, other_row = place(row_ids)
        block_row = dx_row * 2 + other_row
        slot_row = jnp.where(rank_row < ROWS, block_row * ROWS + rank_row, -1)
        pick = jnp.where(sub == slot_row, 1.0, 0.0).astype(BF16)
        spill_row = jnp.where(rank_row == ROWS, block_row, -1)
        spill_sub = lax.broadcasted_iota(jnp.int32, (16, toks), 0)
        pick_spill = jnp.where(spill_sub == spill_row, 1.0, 0.0).astype(BF16)
        dx_col, other_col = place(col_ids)
        first = jnp.where(other_col == 1, 0, 12) + dx_col
        second = jnp.where(other_col == 1, 2 - twist, 1 + twist) * 4 + dx_col
        plain = rank_col < ROWS
        wide = lax.broadcasted_iota(jnp.int32, (toks, HALF * ROWS), 1)
        narrow = lax.broadcasted_iota(jnp.int32, (toks, HALF), 1)
        puts, put_spills = [], []
        for part in range(2):
            begin = part * HALF
            put, put_spill = 0.0, 0.0
            for block in (first, second):
                inside = (block >= begin) & (block < begin + HALF)
                slot = jnp.where(plain & inside, (block - begin) * ROWS + rank_col, -1)
                put = put + jnp.where(wide == slot, 1.0, 0.0)
                slot = jnp.where(plain, -1, block - begin)
                put_spill = put_spill + jnp.where(narrow == slot, 1.0, 0.0)
            puts.append(put.astype(BF16))
            put_spills.append(put_spill.astype(BF16))
        weight = column(mix[step : step + 1, :])
        return pick, pick_spill, puts, put_spills, weight

    def dot(a, b):
        return jnp.dot(a, b, preferred_element_type=F32)

    def dot_t(a, b):
        return lax.dot_general(a, b, (((1,), (1,)), ((), ())), preferred_element_type=F32)

    def fold_rows(value, buffer):
        for c in range(chunks):
            fold[c // 8, pl.ds(c % 8, 8, stride=8), :] = value[:8, c * LANES : (c + 1) * LANES]
        for c in range(chunks, folds * 8):
            fold[c // 8, pl.ds(c % 8, 8, stride=8), :] = jnp.zeros((8, LANES), F32)
        for b in range(folds):
            buffer[:, width + b * LANES : width + (b + 1) * LANES] = fold[b].astype(BF16)

    def unfold_rows(buffer):
        for b in range(folds):
            fold[b] = buffer[:, width + b * LANES : width + (b + 1) * LANES].astype(F32)
        return jnp.concatenate([fold[c // 8, pl.ds(c % 8, 8, stride=8), :] for c in range(chunks)], axis=1)

    def pack(ex, step_plan, values):
        pick, pick_spill, _, _, _ = step_plan
        buffer = sends.at[ex]
        buffer[:, :width] = dot(pick, values).astype(BF16)
        fold_rows(dot(pick_spill, values), buffer)
        recvs[ex, SELF * ROWS : (SELF + 1) * ROWS, :] = sends[ex, 0:ROWS, :]

    def part_rows(part):
        return slice(part * HALF * ROWS, (part + 1) * HALF * ROWS)

    def arrived(ex, part):
        each(dispatch_copy, ex, "recv", PARTS[part])
        buffer = recvs.at[ex, part_rows(part), :]
        x_all[part, 0 : HALF * ROWS, :] = buffer[:, :width]
        x_all[part, HALF * ROWS : HALF * ROWS + 8, :] = unfold_rows(buffer).astype(BF16)

    def send_back(ex, part, value, start):
        buffer = back_sends.at[ex, part_rows(part), :]
        buffer[:, :width] = value[: HALF * ROWS].astype(BF16)
        fold_rows(value[HALF * ROWS :], buffer)
        if start:
            each(back_copy, ex, "start", PARTS[part])
        if part == 1:
            back_recvs[ex, SELF * ROWS : (SELF + 1) * ROWS, :] = back_sends[ex, SELF * ROWS : (SELF + 1) * ROWS, :]

    def collected(ex, step_plan, then=None):
        _, _, puts, put_spills, weight = step_plan
        total = None
        for part in (1, 0):
            each(back_copy, ex, "recv", PARTS[part])
            if part == 0 and then is not None:
                then()
            buffer = back_recvs.at[ex, part_rows(part), :]
            spill = unfold_rows(buffer).astype(BF16)
            term = dot(puts[part], buffer[:, :width]) + dot(put_spills[part], spill)
            total = term if total is None else total + term
        return weight * total

    def project(step, part):
        gates[step, part] = dot_t(x_all[part], wg[...])
        uppers[step, part] = dot_t(x_all[part], wu[...])

    def activate(step, part):
        gate = gates[step, part]
        return (gate * jax.nn.sigmoid(gate) * uppers[step, part]).astype(BF16)

    def derive(step, part):
        d_inner = dot_t(x_all[part], wd[...])
        gate = gates[step, part]
        r = jax.nn.sigmoid(gate)
        d_gate = (d_inner * uppers[step, part] * r * (1.0 + gate * (1.0 - r))).astype(BF16)
        d_upper = (d_inner * gate * r).astype(BF16)
        return dot(d_gate, wg[...]) + dot(d_upper, wu[...])

    def inv_scale(values):
        return lax.rsqrt(jnp.mean(values * values, axis=-1, keepdims=True) + EPSILON)

    def normed(hidden):
        values = hidden.astype(F32)
        return (values * inv_scale(values) * gain[...]).astype(BF16)

    def pulled(hidden, grad, d_normed):
        values = hidden.astype(F32)
        r = inv_scale(values)
        scaled = d_normed * gain[...]
        mean = jnp.mean(scaled * values, axis=-1, keepdims=True)
        return grad.astype(F32) + r * scaled - values * (r * r * r * mean)

    plan0 = plan(0)
    pack(0, plan0, normed(tokens[...]))
    pl.semaphore_wait(barrier, NB + 3 + 3)
    weight_copy(0).start()
    weight_copy(1).start()
    each(dispatch_copy, 0, "start", ALL)
    plan1 = plan(1)
    pack(1, plan1, cotangent[...])
    each(dispatch_copy, 1, "start", NEAR)
    for n in range(3):
        weight_local(n).start()
    x_all[:, HALF * ROWS + 8 :, :] = jnp.zeros((2, 8, width), BF16)
    arrived(0, 1)
    arrived(0, 0)
    weight_copy(2).start()
    for n in range(3):
        weight_local(n).wait()
    weight_copy(0).wait_recv()
    weight_copy(1).wait_recv()
    project(0, 0)
    project(0, 1)
    far, near = activate(0, 0), activate(0, 1)
    weight_copy(2).wait_recv()
    each(dispatch_copy, 1, "start", MIDDLE)
    send_back(0, 0, dot(far, wd[...]), True)
    send_back(0, 1, dot(near, wd[...]), True)
    combined = collected(0, plan0, lambda: each(dispatch_copy, 1, "start", LAST))
    hop_out[0] = (tokens[...].astype(F32) + combined).astype(BF16)
    hop_copy(0).start()
    hop_copy(0).wait_recv()
    hidden1[...] = hop_in[0]
    pack(2, plan1, normed(hidden1[...]))
    each(dispatch_copy, 2, "start", ALL)
    arrived(2, 1)
    project(1, 1)
    arrived(1, 1)
    send_back(1, 1, derive(1, 1), True)
    send_back(2, 1, dot(activate(1, 1), wd[...]), False)
    arrived(2, 0)
    each(back_copy, 2, "start", NEAR)
    project(1, 0)
    arrived(1, 0)
    send_back(1, 0, derive(1, 0), True)
    send_back(2, 0, dot(activate(1, 0), wd[...]), False)
    d_normed = collected(1, plan1, lambda: each(back_copy, 2, "start", LAST))
    hop_out[1] = pulled(hidden1[...], cotangent[...], d_normed).astype(BF16)
    hop_copy(1).start()
    hop_copy(1).wait_recv()
    pack(3, plan0, hop_in[1])
    each(dispatch_copy, 3, "start", ALL)
    arrived(3, 1)
    send_back(3, 1, derive(0, 1), True)
    arrived(3, 0)
    each(back_copy, 2, "start", MIDDLE)
    send_back(3, 0, derive(0, 0), True)
    final[...] = (hidden1[...].astype(F32) + collected(2, plan1)).astype(BF16)
    grads[...] = pulled(tokens[...], hop_in[1], collected(3, plan0)).astype(BF16)

    for ex in range(4):
        each(dispatch_copy, ex, "sent", ALL)
        each(back_copy, ex, "sent", ALL)
    for n in range(3):
        weight_copy(n).wait_send()
    for n in range(2):
        hop_copy(n).wait_send()


def local(tokens, norm_gain, w_gate, w_up, w_down, routes, mix_weights, cotangent):
    toks, width = tokens.shape[1:]
    hid = w_gate.shape[3]
    lanes = width + 3 * LANES
    rows = HALF * (ROWS + 2)
    dma = pltpu.SemaphoreType.DMA
    vmem = pl.BlockSpec(memory_space=pltpu.VMEM)
    anywhere = pl.BlockSpec(memory_space=pl.ANY)
    out = jax.ShapeDtypeStruct((toks, width), BF16)
    final, grads = pl.pallas_call(
        kernel,
        out_shape=(out, out),
        in_specs=[vmem] * 2 + [anywhere] * 3 + [vmem] * 3,
        out_specs=(vmem, vmem),
        scratch_shapes=[
            pltpu.VMEM((2 * hid, width), BF16),
            pltpu.VMEM((2 * hid, width), BF16),
            pltpu.VMEM((2 * hid, width), BF16),
            pltpu.VMEM((4, 8 * ROWS, lanes), BF16),
            pltpu.VMEM((4, NB * ROWS, lanes), BF16),
            pltpu.VMEM((4, NB * ROWS, lanes), BF16),
            pltpu.VMEM((4, NB * ROWS, lanes), BF16),
            pltpu.VMEM((3, HALF * ROWS, LANES), F32),
            pltpu.VMEM((2, rows, width), BF16),
            pltpu.VMEM((2, 2, rows, 2 * hid), F32),
            pltpu.VMEM((2, 2, rows, 2 * hid), F32),
            pltpu.VMEM((toks, width), BF16),
            pltpu.VMEM((2, toks, width), BF16),
            pltpu.VMEM((2, toks, width), BF16),
            dma((4, NB)),
            dma((4, NB)),
            dma((4, NB)),
            dma((4, NB)),
            dma((3,)),
            dma((3,)),
            dma((3,)),
            dma((2,)),
            dma((2,)),
        ],
        compiler_params=pltpu.CompilerParams(
            collective_id=0, has_side_effects=True, vmem_limit_bytes=56 * 1024 * 1024
        ),
    )(
        tokens[0], norm_gain, w_gate[0, 0].T, w_up[0, 0].T, w_down[0, 0],
        routes[0, :, :, 0], mix_weights[0, :, :, 0], cotangent[0],
    )
    return final[None], grads[None]


def solution(mesh):
    in_specs = (
        P("section", "expert", None),
        P("section", None),
        P("section", "expert", None, None),
        P("section", "expert", None, None),
        P("section", "expert", None, None),
        P("section", None, "expert", None),
        P("section", None, "expert", None),
        P("section", "expert", None),
    )
    out_specs = (P("section", "expert", None), P("section", "expert", None))
    return jax.shard_map(local, mesh=mesh, in_specs=in_specs, out_specs=out_specs, check_vma=False)
```

```python
import jax
import jax.numpy as jnp
from jax import lax
from jax.experimental import pallas as pl
from jax.experimental.pallas import tpu as pltpu
from jax.sharding import PartitionSpec as P

MESH = pl.DeviceIdType.MESH
EPSILON = 1e-06
F32 = jnp.float32
BF16 = jnp.bfloat16
XS = 4
ZS = 8
NB = 16
ROWS = 8
LANES = 128
SELF = 12
FAR, NEAR = ((0, 8),), ((8, SELF), (SELF + 1, NB))
ALL = ((0, SELF), (SELF + 1, NB))
PARTS = (FAR, NEAR)
LAST, MIDDLE = ((0, 4),), ((4, 8),)
HALF = 8


def kernel(
    tokens, gain, w_gate, w_up, w_down, routes, mix, cotangent, final, grads,
    wg, wu, wd, sends, recvs, back_sends, back_recvs, fold, x_all, gates, uppers, hidden1,
    hop_out, hop_in,
    send_sems, recv_sems, bsend_sems, brecv_sems, w_local, w_send, w_recv, hop_send, hop_recv,
):
    width = tokens.shape[1]
    toks = tokens.shape[0]
    hid = w_gate.shape[0]
    chunks = width // LANES
    folds = -(-chunks // 8)
    section = lax.axis_index("section")
    sections = lax.axis_size("section")
    me = lax.axis_index("expert")
    x = me // ZS
    z = me % ZS
    sign = 1 - 2 * (z % 2)
    own_half = z // 4
    twist = ((z + 1) // 2) % 2

    def at(xd, zd):
        return {"expert": ((xd + XS) % XS) * ZS + (zd + 2 * ZS) % ZS}

    def target(i):
        j = i // 4
        off = (j - 3) * (1 - 2 * (j % 2))
        return x + i % 4, (z + off * sign + ZS) % ZS

    def origin(i):
        return x - i % 4, (z + (i // 4 - 3) * sign + ZS) % ZS

    partner = at(x, z + sign)
    after = {"section": (section + 1) % sections}
    before = {"section": (section + sections - 1) % sections}

    def weight_local(n):
        src, dst = ((w_gate, wg), (w_up, wu), (w_down, wd))[n]
        return pltpu.make_async_copy(src, dst.at[0:hid, :], w_local.at[n])

    def weight_copy(n):
        src, dst = ((w_gate, wg), (w_up, wu), (w_down, wd))[n]
        return pltpu.make_async_remote_copy(
            src_ref=src, dst_ref=dst.at[hid : 2 * hid, :], send_sem=w_send.at[n], recv_sem=w_recv.at[n],
            device_id=partner, device_id_type=MESH,
        )

    def hop_rows(h):
        return slice(h * toks // 2, (h + 1) * toks // 2)

    def hop_copy(n, h):
        rows = hop_rows(h)
        return pltpu.make_async_remote_copy(
            src_ref=hop_out.at[n, rows, :], dst_ref=hop_in.at[n, rows, :], send_sem=hop_send.at[n, h], recv_sem=hop_recv.at[n, h],
            device_id=after if n == 0 else before, device_id_type=MESH,
        )

    def over(ranges, action):
        def body(i, carry):
            action(i)
            return carry

        for low, high in ranges:
            lax.fori_loop(low, high, body, 0)

    barrier = pltpu.get_barrier_semaphore()

    def greet(i):
        j = i // 4
        zd = z + (j - 3 + j // 4) * sign
        pl.semaphore_signal(barrier, inc=1, device_id=at(x + i % 4, zd), device_id_type=MESH)

    over(((0, SELF), (SELF + 1, NB + 4)), greet)
    for neighbour in (partner, after, before):
        pl.semaphore_signal(barrier, inc=1, device_id=neighbour, device_id_type=MESH)

    def dispatch_copy(ex, i):
        xd, zd = target(i)
        block = (i % 4) * 2 + (zd // 4 + own_half) % 2
        return pltpu.make_async_remote_copy(
            src_ref=sends.at[ex, pl.ds(pl.multiple_of(block * ROWS, ROWS), ROWS), :],
            dst_ref=recvs.at[ex, pl.ds(pl.multiple_of(i * ROWS, ROWS), ROWS), :],
            send_sem=send_sems.at[ex, i],
            recv_sem=recv_sems.at[ex, i],
            device_id=at(xd, zd),
            device_id_type=MESH,
        )

    def back_copy(ex, i):
        xd, zd = origin(i)
        rows = pl.ds(pl.multiple_of(i * ROWS, ROWS), ROWS)
        return pltpu.make_async_remote_copy(
            src_ref=back_sends.at[ex, rows, :],
            dst_ref=back_recvs.at[ex, rows, :],
            send_sem=bsend_sems.at[ex, i],
            recv_sem=brecv_sems.at[ex, i],
            device_id=at(xd, zd),
            device_id_type=MESH,
        )

    def each(copy_of, ex, action, ranges):
        def one(i):
            copy = copy_of(ex, i)
            if action == "start":
                copy.start()
            elif action == "recv":
                copy.wait_recv()
            else:
                copy.wait_send()

        over(ranges, one)

    sub = lax.broadcasted_iota(jnp.int32, (toks, toks), 0)
    lane = lax.broadcasted_iota(jnp.int32, (toks, toks), 1)

    def column(row):
        return jnp.sum(jnp.where(sub == lane, jnp.broadcast_to(row, (toks, toks)), 0), axis=1, keepdims=True)

    def place(ids):
        dx = (ids // 2 - x + XS) % XS
        other = (ids % 2 + own_half) % 2
        return dx, other

    def plan(step):
        row_ids = routes[step : step + 1, :]
        col_ids = column(row_ids)
        same = (col_ids == row_ids).astype(jnp.int32)
        rank_col = jnp.sum(jnp.where(lane < sub, same, 0), axis=1, keepdims=True)
        rank_row = jnp.sum(jnp.where(sub < lane, same, 0), axis=0, keepdims=True)
        dx_row, other_row = place(row_ids)
        block_row = dx_row * 2 + other_row
        slot_row = jnp.where(rank_row < ROWS, block_row * ROWS + rank_row, -1)
        pick = jnp.where(sub == slot_row, 1.0, 0.0).astype(BF16)
        spill_row = jnp.where(rank_row == ROWS, block_row, -1)
        spill_sub = lax.broadcasted_iota(jnp.int32, (16, toks), 0)
        pick_spill = jnp.where(spill_sub == spill_row, 1.0, 0.0).astype(BF16)
        dx_col, other_col = place(col_ids)
        first = jnp.where(other_col == 1, 0, 12) + dx_col
        second = jnp.where(other_col == 1, 2 - twist, 1 + twist) * 4 + dx_col
        plain = rank_col < ROWS
        wide = lax.broadcasted_iota(jnp.int32, (toks, HALF * ROWS), 1)
        narrow = lax.broadcasted_iota(jnp.int32, (toks, HALF), 1)
        puts, put_spills = [], []
        for part in range(2):
            begin = part * HALF
            put, put_spill = 0.0, 0.0
            for block in (first, second):
                inside = (block >= begin) & (block < begin + HALF)
                slot = jnp.where(plain & inside, (block - begin) * ROWS + rank_col, -1)
                put = put + jnp.where(wide == slot, 1.0, 0.0)
                slot = jnp.where(plain, -1, block - begin)
                put_spill = put_spill + jnp.where(narrow == slot, 1.0, 0.0)
            puts.append(put.astype(BF16))
            put_spills.append(put_spill.astype(BF16))
        weight = column(mix[step : step + 1, :])
        return pick, pick_spill, puts, put_spills, weight

    def dot(a, b):
        return jnp.dot(a, b, preferred_element_type=F32)

    def dot_t(a, b):
        return lax.dot_general(a, b, (((1,), (1,)), ((), ())), preferred_element_type=F32)

    def fold_rows(value, buffer):
        for c in range(chunks):
            fold[c // 8, pl.ds(c % 8, 8, stride=8), :] = value[:8, c * LANES : (c + 1) * LANES]
        for c in range(chunks, folds * 8):
            fold[c // 8, pl.ds(c % 8, 8, stride=8), :] = jnp.zeros((8, LANES), F32)
        for b in range(folds):
            buffer[:, width + b * LANES : width + (b + 1) * LANES] = fold[b].astype(BF16)

    def unfold_rows(buffer):
        for b in range(folds):
            fold[b] = buffer[:, width + b * LANES : width + (b + 1) * LANES].astype(F32)
        return jnp.concatenate([fold[c // 8, pl.ds(c % 8, 8, stride=8), :] for c in range(chunks)], axis=1)

    def pack(ex, step_plan, values):
        pick, pick_spill, _, _, _ = step_plan
        buffer = sends.at[ex]
        buffer[:, :width] = dot(pick, values).astype(BF16)
        fold_rows(dot(pick_spill, values), buffer)
        recvs[ex, SELF * ROWS : (SELF + 1) * ROWS, :] = sends[ex, 0:ROWS, :]

    def part_rows(part):
        return slice(part * HALF * ROWS, (part + 1) * HALF * ROWS)

    def arrived(ex, part):
        each(dispatch_copy, ex, "recv", PARTS[part])
        buffer = recvs.at[ex, part_rows(part), :]
        x_all[part, 0 : HALF * ROWS, :] = buffer[:, :width]
        x_all[part, HALF * ROWS : HALF * ROWS + 8, :] = unfold_rows(buffer).astype(BF16)

    def send_back(ex, part, value, start):
        buffer = back_sends.at[ex, part_rows(part), :]
        buffer[:, :width] = value[: HALF * ROWS].astype(BF16)
        fold_rows(value[HALF * ROWS :], buffer)
        if start:
            each(back_copy, ex, "start", PARTS[part])
        if part == 1:
            back_recvs[ex, SELF * ROWS : (SELF + 1) * ROWS, :] = back_sends[ex, SELF * ROWS : (SELF + 1) * ROWS, :]

    def collected(ex, step_plan, then, count):
        _, _, puts, put_spills, weight = step_plan
        total = [0.0] * count
        for part in (1, 0):
            each(back_copy, ex, "recv", PARTS[part])
            if part == 0:
                then()
            buffer = back_recvs.at[ex, part_rows(part), :]
            spill = unfold_rows(buffer).astype(BF16)
            for h in range(count):
                rows = slice(h * toks // count, (h + 1) * toks // count)
                total[h] += dot(puts[part][rows], buffer[:, :width]) + dot(put_spills[part][rows], spill)
                if part == 0:
                    yield rows, weight[rows] * total[h]

    def project(step, part):
        gates[step, part] = dot_t(x_all[part], wg[...])
        uppers[step, part] = dot_t(x_all[part], wu[...])

    def activate(step, part):
        gate = gates[step, part]
        return (gate * jax.nn.sigmoid(gate) * uppers[step, part]).astype(BF16)

    def derive(step, part):
        d_inner = dot_t(x_all[part], wd[...])
        gate = gates[step, part]
        r = jax.nn.sigmoid(gate)
        d_gate = (d_inner * uppers[step, part] * r * (1.0 + gate * (1.0 - r))).astype(BF16)
        d_upper = (d_inner * gate * r).astype(BF16)
        return dot(d_gate, wg[...]) + dot(d_upper, wu[...])

    def inv_scale(values):
        return lax.rsqrt(jnp.mean(values * values, axis=-1, keepdims=True) + EPSILON)

    def normed(hidden):
        values = hidden.astype(F32)
        return (values * inv_scale(values) * gain[...]).astype(BF16)

    def pulled(hidden, grad, d_normed):
        values = hidden.astype(F32)
        r = inv_scale(values)
        scaled = d_normed * gain[...]
        mean = jnp.mean(scaled * values, axis=-1, keepdims=True)
        return grad.astype(F32) + r * scaled - values * (r * r * r * mean)

    plan0 = plan(0)
    pack(0, plan0, normed(tokens[...]))
    pl.semaphore_wait(barrier, NB + 3 + 3)
    weight_copy(0).start()
    weight_copy(1).start()
    each(dispatch_copy, 0, "start", ALL)
    plan1 = plan(1)
    pack(1, plan1, cotangent[...])
    each(dispatch_copy, 1, "start", NEAR)
    for n in range(3):
        weight_local(n).start()
    x_all[:, HALF * ROWS + 8 :, :] = jnp.zeros((2, 8, width), BF16)
    arrived(0, 1)
    arrived(0, 0)
    weight_copy(2).start()
    for n in range(3):
        weight_local(n).wait()
    weight_copy(0).wait_recv()
    weight_copy(1).wait_recv()
    project(0, 0)
    project(0, 1)
    far, near = activate(0, 0), activate(0, 1)
    weight_copy(2).wait_recv()
    each(dispatch_copy, 1, "start", MIDDLE)
    send_back(0, 0, dot(far, wd[...]), True)
    send_back(0, 1, dot(near, wd[...]), True)
    for h, (rows, combined) in enumerate(collected(0, plan0, lambda: each(dispatch_copy, 1, "start", LAST), 2)):
        hop_out[0, rows, :] = (tokens[rows, :].astype(F32) + combined).astype(BF16)
        hop_copy(0, h).start()
    for h in range(2):
        hop_copy(0, h).wait_recv()
        hidden1[hop_rows(h), :] = normed(hop_in[0, hop_rows(h), :])
    pack(2, plan1, hidden1[...])
    hidden1[...] = hop_in[0]
    each(dispatch_copy, 2, "start", ALL)
    arrived(2, 1)
    project(1, 1)
    arrived(1, 1)
    send_back(1, 1, derive(1, 1), True)
    send_back(2, 1, dot(activate(1, 1), wd[...]), False)
    arrived(2, 0)
    each(back_copy, 2, "start", NEAR)
    project(1, 0)
    arrived(1, 0)
    send_back(1, 0, derive(1, 0), True)
    send_back(2, 0, dot(activate(1, 0), wd[...]), False)
    for h, (rows, d_normed) in enumerate(collected(1, plan1, lambda: each(back_copy, 2, "start", LAST), 2)):
        hop_out[1, rows, :] = pulled(hidden1[rows, :], cotangent[rows, :], d_normed).astype(BF16)
        hop_copy(1, h).start()
    for h in range(2):
        hop_copy(1, h).wait_recv()
    pack(3, plan0, hop_in[1])
    each(dispatch_copy, 3, "start", ALL)
    arrived(3, 1)
    send_back(3, 1, derive(0, 1), True)
    arrived(3, 0)
    each(back_copy, 2, "start", MIDDLE)
    send_back(3, 0, derive(0, 0), True)
    for rows, combined in collected(2, plan1, lambda: None, 1):
        final[rows, :] = (hidden1[rows, :].astype(F32) + combined).astype(BF16)
    for rows, d_normed in collected(3, plan0, lambda: None, 1):
        grads[rows, :] = pulled(tokens[rows, :], hop_in[1, rows, :], d_normed).astype(BF16)

    for ex in range(4):
        each(dispatch_copy, ex, "sent", ALL)
        each(back_copy, ex, "sent", ALL)
    for n in range(3):
        weight_copy(n).wait_send()
    for n in range(2):
        for h in range(2):
            hop_copy(n, h).wait_send()


def local(tokens, norm_gain, w_gate, w_up, w_down, routes, mix_weights, cotangent):
    toks, width = tokens.shape[1:]
    hid = w_gate.shape[3]
    lanes = width + 3 * LANES
    rows = HALF * (ROWS + 2)
    dma = pltpu.SemaphoreType.DMA
    vmem = pl.BlockSpec(memory_space=pltpu.VMEM)
    anywhere = pl.BlockSpec(memory_space=pl.ANY)
    out = jax.ShapeDtypeStruct((toks, width), BF16)
    final, grads = pl.pallas_call(
        kernel,
        out_shape=(out, out),
        in_specs=[vmem] * 2 + [anywhere] * 3 + [vmem] * 3,
        out_specs=(vmem, vmem),
        scratch_shapes=[
            pltpu.VMEM((2 * hid, width), BF16),
            pltpu.VMEM((2 * hid, width), BF16),
            pltpu.VMEM((2 * hid, width), BF16),
            pltpu.VMEM((4, 8 * ROWS, lanes), BF16),
            pltpu.VMEM((4, NB * ROWS, lanes), BF16),
            pltpu.VMEM((4, NB * ROWS, lanes), BF16),
            pltpu.VMEM((4, NB * ROWS, lanes), BF16),
            pltpu.VMEM((3, HALF * ROWS, LANES), F32),
            pltpu.VMEM((2, rows, width), BF16),
            pltpu.VMEM((2, 2, rows, 2 * hid), F32),
            pltpu.VMEM((2, 2, rows, 2 * hid), F32),
            pltpu.VMEM((toks, width), BF16),
            pltpu.VMEM((2, toks, width), BF16),
            pltpu.VMEM((2, toks, width), BF16),
            dma((4, NB)),
            dma((4, NB)),
            dma((4, NB)),
            dma((4, NB)),
            dma((3,)),
            dma((3,)),
            dma((3,)),
            dma((2, 2)),
            dma((2, 2)),
        ],
        compiler_params=pltpu.CompilerParams(
            collective_id=0, has_side_effects=True, vmem_limit_bytes=56 * 1024 * 1024
        ),
    )(
        tokens[0], norm_gain, w_gate[0, 0].T, w_up[0, 0].T, w_down[0, 0],
        routes[0, :, :, 0], mix_weights[0, :, :, 0], cotangent[0],
    )
    return final[None], grads[None]


def solution(mesh):
    in_specs = (
        P("section", "expert", None),
        P("section", None),
        P("section", "expert", None, None),
        P("section", "expert", None, None),
        P("section", "expert", None, None),
        P("section", None, "expert", None),
        P("section", None, "expert", None),
        P("section", "expert", None),
    )
    out_specs = (P("section", "expert", None), P("section", "expert", None))
    return jax.shard_map(local, mesh=mesh, in_specs=in_specs, out_specs=out_specs, check_vma=False)
```

```python
import jax
import jax.numpy as jnp
from jax import lax
from jax.experimental import pallas as pl
from jax.experimental.pallas import tpu as pltpu
from jax.sharding import PartitionSpec as P

MESH = pl.DeviceIdType.MESH
EPSILON = 1e-06
F32 = jnp.float32
BF16 = jnp.bfloat16
XS = 4
ZS = 8
NB = 16
ROWS = 8
LANES = 128
SELF = 12
FAR, NEAR = ((0, 8),), ((8, SELF), (SELF + 1, NB))
ALL = ((0, SELF), (SELF + 1, NB))
PARTS = (FAR, NEAR)
LAST, MIDDLE = ((0, 4),), ((4, 8),)
HALF = 8


def kernel(
    tokens, gain, w_gate, w_up, w_down, routes, mix, cotangent, final, grads,
    wg, wu, wd, sends, recvs, back_sends, back_recvs, fold, x_all, gates, uppers, hidden1,
    hop_out, hop_in,
    send_sems, recv_sems, bsend_sems, brecv_sems, w_local, w_send, w_recv, hop_send, hop_recv,
):
    width = tokens.shape[1]
    toks = tokens.shape[0]
    hid = w_gate.shape[0]
    chunks = width // LANES
    folds = -(-chunks // 8)
    section = lax.axis_index("section")
    sections = lax.axis_size("section")
    me = lax.axis_index("expert")
    x = me // ZS
    z = me % ZS
    sign = 1 - 2 * (z % 2)
    own_half = z // 4
    twist = ((z + 1) // 2) % 2

    def at(xd, zd):
        return {"expert": ((xd + XS) % XS) * ZS + (zd + 2 * ZS) % ZS}

    def target(i):
        j = i // 4
        off = (j - 3) * (1 - 2 * (j % 2))
        return x + i % 4, (z + off * sign + ZS) % ZS

    def origin(i):
        return x - i % 4, (z + (i // 4 - 3) * sign + ZS) % ZS

    partner = at(x, z + sign)
    after = {"section": (section + 1) % sections}
    before = {"section": (section + sections - 1) % sections}

    def weight_local(n):
        src, dst = ((w_gate, wg), (w_up, wu), (w_down, wd))[n]
        return pltpu.make_async_copy(src, dst.at[0:hid, :], w_local.at[n])

    def weight_copy(n):
        src, dst = ((w_gate, wg), (w_up, wu), (w_down, wd))[n]
        return pltpu.make_async_remote_copy(
            src_ref=src, dst_ref=dst.at[hid : 2 * hid, :], send_sem=w_send.at[n], recv_sem=w_recv.at[n],
            device_id=partner, device_id_type=MESH,
        )

    def hop_rows(h):
        return slice(h * toks // 2, (h + 1) * toks // 2)

    def hop_copy(n, h):
        rows = hop_rows(h)
        return pltpu.make_async_remote_copy(
            src_ref=hop_out.at[n, rows, :], dst_ref=hop_in.at[n, rows, :], send_sem=hop_send.at[n, h], recv_sem=hop_recv.at[n, h],
            device_id=after if n == 0 else before, device_id_type=MESH,
        )

    def over(ranges, action):
        def body(i, carry):
            action(i)
            return carry

        for low, high in ranges:
            lax.fori_loop(low, high, body, 0)

    barrier = pltpu.get_barrier_semaphore()

    def greet(i):
        j = i // 4
        zd = z + (j - 3 + j // 4) * sign
        pl.semaphore_signal(barrier, inc=1, device_id=at(x + i % 4, zd), device_id_type=MESH)

    over(((0, SELF), (SELF + 1, NB + 4)), greet)
    for neighbour in (partner, after, before):
        pl.semaphore_signal(barrier, inc=1, device_id=neighbour, device_id_type=MESH)

    def dispatch_copy(ex, i):
        xd, zd = target(i)
        block = (i % 4) * 2 + (zd // 4 + own_half) % 2
        return pltpu.make_async_remote_copy(
            src_ref=sends.at[ex, pl.ds(pl.multiple_of(block * ROWS, ROWS), ROWS), :],
            dst_ref=recvs.at[ex, pl.ds(pl.multiple_of(i * ROWS, ROWS), ROWS), :],
            send_sem=send_sems.at[ex, i],
            recv_sem=recv_sems.at[ex, i],
            device_id=at(xd, zd),
            device_id_type=MESH,
        )

    def back_copy(ex, i):
        xd, zd = origin(i)
        rows = pl.ds(pl.multiple_of(i * ROWS, ROWS), ROWS)
        return pltpu.make_async_remote_copy(
            src_ref=back_sends.at[ex, rows, :],
            dst_ref=back_recvs.at[ex, rows, :],
            send_sem=bsend_sems.at[ex, i],
            recv_sem=brecv_sems.at[ex, i],
            device_id=at(xd, zd),
            device_id_type=MESH,
        )

    def each(copy_of, ex, action, ranges):
        def one(i):
            copy = copy_of(ex, i)
            if action == "start":
                copy.start()
            elif action == "recv":
                copy.wait_recv()
            else:
                copy.wait_send()

        over(ranges, one)

    sub = lax.broadcasted_iota(jnp.int32, (toks, toks), 0)
    lane = lax.broadcasted_iota(jnp.int32, (toks, toks), 1)

    def column(row):
        return jnp.sum(jnp.where(sub == lane, jnp.broadcast_to(row, (toks, toks)), 0), axis=1, keepdims=True)

    def place(ids):
        dx = (ids // 2 - x + XS) % XS
        other = (ids % 2 + own_half) % 2
        return dx, other

    def plan(step):
        row_ids = routes[step : step + 1, :]
        col_ids = column(row_ids)
        same = (col_ids == row_ids).astype(jnp.int32)
        rank_col = jnp.sum(jnp.where(lane < sub, same, 0), axis=1, keepdims=True)
        rank_row = jnp.sum(jnp.where(sub < lane, same, 0), axis=0, keepdims=True)
        dx_row, other_row = place(row_ids)
        block_row = dx_row * 2 + other_row
        slot_row = jnp.where(rank_row < ROWS, block_row * ROWS + rank_row, -1)
        pick = jnp.where(sub == slot_row, 1.0, 0.0).astype(BF16)
        spill_row = jnp.where(rank_row == ROWS, block_row, -1)
        spill_sub = lax.broadcasted_iota(jnp.int32, (16, toks), 0)
        pick_spill = jnp.where(spill_sub == spill_row, 1.0, 0.0).astype(BF16)
        dx_col, other_col = place(col_ids)
        first = jnp.where(other_col == 1, 0, 12) + dx_col
        second = jnp.where(other_col == 1, 2 - twist, 1 + twist) * 4 + dx_col
        plain = rank_col < ROWS
        wide = lax.broadcasted_iota(jnp.int32, (toks, HALF * ROWS), 1)
        narrow = lax.broadcasted_iota(jnp.int32, (toks, HALF), 1)
        puts, put_spills = [], []
        for part in range(2):
            begin = part * HALF
            put, put_spill = 0.0, 0.0
            for block in (first, second):
                inside = (block >= begin) & (block < begin + HALF)
                slot = jnp.where(plain & inside, (block - begin) * ROWS + rank_col, -1)
                put = put + jnp.where(wide == slot, 1.0, 0.0)
                slot = jnp.where(plain, -1, block - begin)
                put_spill = put_spill + jnp.where(narrow == slot, 1.0, 0.0)
            puts.append(put.astype(BF16))
            put_spills.append(put_spill.astype(BF16))
        weight = column(mix[step : step + 1, :])
        return pick, pick_spill, puts, put_spills, weight

    def dot(a, b):
        return jnp.dot(a, b, preferred_element_type=F32)

    def dot_t(a, b):
        return lax.dot_general(a, b, (((1,), (1,)), ((), ())), preferred_element_type=F32)

    def fold_rows(value, buffer):
        for c in range(chunks):
            fold[c // 8, pl.ds(c % 8, 8, stride=8), :] = value[:8, c * LANES : (c + 1) * LANES]
        for c in range(chunks, folds * 8):
            fold[c // 8, pl.ds(c % 8, 8, stride=8), :] = jnp.zeros((8, LANES), F32)
        for b in range(folds):
            buffer[:, width + b * LANES : width + (b + 1) * LANES] = fold[b].astype(BF16)

    def unfold_rows(buffer):
        for b in range(folds):
            fold[b] = buffer[:, width + b * LANES : width + (b + 1) * LANES].astype(F32)
        return jnp.concatenate([fold[c // 8, pl.ds(c % 8, 8, stride=8), :] for c in range(chunks)], axis=1)

    def pack(ex, step_plan, values):
        pick, pick_spill, _, _, _ = step_plan
        buffer = sends.at[ex]
        buffer[:, :width] = dot(pick, values).astype(BF16)
        fold_rows(dot(pick_spill, values), buffer)
        recvs[ex, SELF * ROWS : (SELF + 1) * ROWS, :] = sends[ex, 0:ROWS, :]

    def part_rows(part):
        return slice(part * HALF * ROWS, (part + 1) * HALF * ROWS)

    def arrived(ex, part):
        each(dispatch_copy, ex, "recv", PARTS[part])
        buffer = recvs.at[ex, part_rows(part), :]
        x_all[part, 0 : HALF * ROWS, :] = buffer[:, :width]
        x_all[part, HALF * ROWS : HALF * ROWS + 8, :] = unfold_rows(buffer).astype(BF16)

    def send_back(ex, part, value, start):
        buffer = back_sends.at[ex, part_rows(part), :]
        buffer[:, :width] = value[: HALF * ROWS].astype(BF16)
        fold_rows(value[HALF * ROWS :], buffer)
        if start:
            each(back_copy, ex, "start", PARTS[part])
        if part == 1:
            back_recvs[ex, SELF * ROWS : (SELF + 1) * ROWS, :] = back_sends[ex, SELF * ROWS : (SELF + 1) * ROWS, :]

    def collected(ex, step_plan, then, count):
        _, _, puts, put_spills, weight = step_plan
        total = [0.0] * count
        for part in (1, 0):
            each(back_copy, ex, "recv", PARTS[part])
            if part == 0:
                then()
            buffer = back_recvs.at[ex, part_rows(part), :]
            spill = unfold_rows(buffer).astype(BF16)
            for h in range(count):
                rows = slice(h * toks // count, (h + 1) * toks // count)
                total[h] += dot(puts[part][rows], buffer[:, :width]) + dot(put_spills[part][rows], spill)
                if part == 0:
                    yield rows, weight[rows] * total[h]

    def project(step, part):
        gates[step, part] = dot_t(x_all[part], wg[...])
        uppers[step, part] = dot_t(x_all[part], wu[...])

    def activate(step, part):
        gate = gates[step, part]
        return (gate * jax.nn.sigmoid(gate) * uppers[step, part]).astype(BF16)

    def pushed(part):
        return dot_t(x_all[part], wd[...])

    def derive(step, part, d_inner):
        gate = gates[step, part]
        r = jax.nn.sigmoid(gate)
        d_gate = (d_inner * uppers[step, part] * r * (1.0 + gate * (1.0 - r))).astype(BF16)
        d_upper = (d_inner * gate * r).astype(BF16)
        return dot(d_gate, wg[...]) + dot(d_upper, wu[...])

    def inv_scale(values):
        return lax.rsqrt(jnp.mean(values * values, axis=-1, keepdims=True) + EPSILON)

    def normed(hidden):
        values = hidden.astype(F32)
        return (values * inv_scale(values) * gain[...]).astype(BF16)

    def pulled(hidden, r, grad, d_normed):
        values = hidden.astype(F32)
        scaled = d_normed * gain[...]
        mean = jnp.mean(scaled * values, axis=-1, keepdims=True)
        return grad.astype(F32) + r * scaled - values * (r * r * r * mean)

    plan0 = plan(0)
    pack(0, plan0, normed(tokens[...]))
    pl.semaphore_wait(barrier, NB + 3 + 3)
    weight_copy(0).start()
    weight_copy(1).start()
    each(dispatch_copy, 0, "start", ALL)
    plan1 = plan(1)
    pack(1, plan1, cotangent[...])
    each(dispatch_copy, 1, "start", NEAR)
    for n in range(3):
        weight_local(n).start()
    x_all[:, HALF * ROWS + 8 :, :] = jnp.zeros((2, 8, width), BF16)
    arrived(0, 1)
    arrived(0, 0)
    weight_copy(2).start()
    for n in range(3):
        weight_local(n).wait()
    weight_copy(0).wait_recv()
    weight_copy(1).wait_recv()
    project(0, 0)
    project(0, 1)
    far, near = activate(0, 0), activate(0, 1)
    weight_copy(2).wait_recv()
    each(dispatch_copy, 1, "start", MIDDLE)
    send_back(0, 0, dot(far, wd[...]), True)
    send_back(0, 1, dot(near, wd[...]), True)
    for h, (rows, combined) in enumerate(collected(0, plan0, lambda: each(dispatch_copy, 1, "start", LAST), 2)):
        hop_out[0, rows, :] = (tokens[rows, :].astype(F32) + combined).astype(BF16)
        hop_copy(0, h).start()
    for h in range(2):
        hop_copy(0, h).wait_recv()
        hidden1[hop_rows(h), :] = normed(hop_in[0, hop_rows(h), :])
    pack(2, plan1, hidden1[...])
    hidden1[...] = hop_in[0]
    each(dispatch_copy, 2, "start", ALL)
    root1 = inv_scale(hidden1[...].astype(F32))
    arrived(1, 1)
    d_near = pushed(1)
    arrived(2, 1)
    project(1, 1)
    send_back(1, 1, derive(1, 1, d_near), True)
    send_back(2, 1, dot(activate(1, 1), wd[...]), False)
    arrived(1, 0)
    d_far = pushed(0)
    arrived(2, 0)
    each(back_copy, 2, "start", NEAR)
    project(1, 0)
    send_back(1, 0, derive(1, 0, d_far), True)
    send_back(2, 0, dot(activate(1, 0), wd[...]), False)
    for h, (rows, d_normed) in enumerate(collected(1, plan1, lambda: each(back_copy, 2, "start", LAST), 2)):
        hop_out[1, rows, :] = pulled(hidden1[rows, :], root1[rows], cotangent[rows, :], d_normed).astype(BF16)
        hop_copy(1, h).start()
    for h in range(2):
        hop_copy(1, h).wait_recv()
    pack(3, plan0, hop_in[1])
    each(dispatch_copy, 3, "start", ALL)
    arrived(3, 1)
    send_back(3, 1, derive(0, 1, pushed(1)), True)
    arrived(3, 0)
    each(back_copy, 2, "start", MIDDLE)
    send_back(3, 0, derive(0, 0, pushed(0)), True)
    for rows, combined in collected(2, plan1, lambda: None, 1):
        final[rows, :] = (hidden1[rows, :].astype(F32) + combined).astype(BF16)
    root0 = inv_scale(tokens[...].astype(F32))
    for rows, d_normed in collected(3, plan0, lambda: None, 1):
        grads[rows, :] = pulled(tokens[rows, :], root0[rows], hop_in[1, rows, :], d_normed).astype(BF16)

    for ex in range(4):
        each(dispatch_copy, ex, "sent", ALL)
        each(back_copy, ex, "sent", ALL)
    for n in range(3):
        weight_copy(n).wait_send()
    for n in range(2):
        for h in range(2):
            hop_copy(n, h).wait_send()


def local(tokens, norm_gain, w_gate, w_up, w_down, routes, mix_weights, cotangent):
    toks, width = tokens.shape[1:]
    hid = w_gate.shape[3]
    lanes = width + 3 * LANES
    rows = HALF * (ROWS + 2)
    dma = pltpu.SemaphoreType.DMA
    vmem = pl.BlockSpec(memory_space=pltpu.VMEM)
    anywhere = pl.BlockSpec(memory_space=pl.ANY)
    out = jax.ShapeDtypeStruct((toks, width), BF16)
    final, grads = pl.pallas_call(
        kernel,
        out_shape=(out, out),
        in_specs=[vmem] * 2 + [anywhere] * 3 + [vmem] * 3,
        out_specs=(vmem, vmem),
        scratch_shapes=[
            pltpu.VMEM((2 * hid, width), BF16),
            pltpu.VMEM((2 * hid, width), BF16),
            pltpu.VMEM((2 * hid, width), BF16),
            pltpu.VMEM((4, 8 * ROWS, lanes), BF16),
            pltpu.VMEM((4, NB * ROWS, lanes), BF16),
            pltpu.VMEM((4, NB * ROWS, lanes), BF16),
            pltpu.VMEM((4, NB * ROWS, lanes), BF16),
            pltpu.VMEM((3, HALF * ROWS, LANES), F32),
            pltpu.VMEM((2, rows, width), BF16),
            pltpu.VMEM((2, 2, rows, 2 * hid), F32),
            pltpu.VMEM((2, 2, rows, 2 * hid), F32),
            pltpu.VMEM((toks, width), BF16),
            pltpu.VMEM((2, toks, width), BF16),
            pltpu.VMEM((2, toks, width), BF16),
            dma((4, NB)),
            dma((4, NB)),
            dma((4, NB)),
            dma((4, NB)),
            dma((3,)),
            dma((3,)),
            dma((3,)),
            dma((2, 2)),
            dma((2, 2)),
        ],
        compiler_params=pltpu.CompilerParams(
            collective_id=0, has_side_effects=True, vmem_limit_bytes=56 * 1024 * 1024
        ),
    )(
        tokens[0], norm_gain, w_gate[0, 0].T, w_up[0, 0].T, w_down[0, 0],
        routes[0, :, :, 0], mix_weights[0, :, :, 0], cotangent[0],
    )
    return final[None], grads[None]


def solution(mesh):
    in_specs = (
        P("section", "expert", None),
        P("section", None),
        P("section", "expert", None, None),
        P("section", "expert", None, None),
        P("section", "expert", None, None),
        P("section", None, "expert", None),
        P("section", None, "expert", None),
        P("section", "expert", None),
    )
    out_specs = (P("section", "expert", None), P("section", "expert", None))
    return jax.shard_map(local, mesh=mesh, in_specs=in_specs, out_specs=out_specs, check_vma=False)
```

```python
import jax
import jax.numpy as jnp
from jax import lax
from jax.experimental import pallas as pl
from jax.experimental.pallas import tpu as pltpu
from jax.sharding import PartitionSpec as P

MESH = pl.DeviceIdType.MESH
EPSILON = 1e-06
F32 = jnp.float32
BF16 = jnp.bfloat16
XS = 4
ZS = 8
NB = 16
ROWS = 8
LANES = 128
SELF = 12
FAR, NEAR = ((0, 8),), ((8, SELF), (SELF + 1, NB))
ALL = ((0, SELF), (SELF + 1, NB))
PARTS = (FAR, NEAR)
LAST, MIDDLE = ((0, 4),), ((4, 8),)
HALF = 8


def kernel(
    tokens, gain, w_gate, w_up, w_down, routes, mix, cotangent, final, grads,
    wg, wu, wd, sends, recvs, back_sends, back_recvs, fold, x_all, gates, uppers, hidden1,
    hop_out, hop_in,
    send_sems, recv_sems, bsend_sems, brecv_sems, w_local, w_send, w_recv, hop_send, hop_recv,
):
    width = tokens.shape[1]
    toks = tokens.shape[0]
    hid = w_gate.shape[0]
    chunks = width // LANES
    folds = -(-chunks // 8)
    section = lax.axis_index("section")
    sections = lax.axis_size("section")
    me = lax.axis_index("expert")
    x = me // ZS
    z = me % ZS
    sign = 1 - 2 * (z % 2)
    own_half = z // 4
    twist = ((z + 1) // 2) % 2

    def at(xd, zd):
        return {"expert": ((xd + XS) % XS) * ZS + (zd + 2 * ZS) % ZS}

    def target(i):
        j = i // 4
        off = (j - 3) * (1 - 2 * (j % 2))
        return x + i % 4, (z + off * sign + ZS) % ZS

    def origin(i):
        return x - i % 4, (z + (i // 4 - 3) * sign + ZS) % ZS

    partner = at(x, z + sign)
    after = {"section": (section + 1) % sections}
    before = {"section": (section + sections - 1) % sections}

    def weight_local(n):
        src, dst = ((w_gate, wg), (w_up, wu), (w_down, wd))[n]
        return pltpu.make_async_copy(src, dst.at[0:hid, :], w_local.at[n])

    def weight_copy(n):
        src, dst = ((w_gate, wg), (w_up, wu), (w_down, wd))[n]
        return pltpu.make_async_remote_copy(
            src_ref=src, dst_ref=dst.at[hid : 2 * hid, :], send_sem=w_send.at[n], recv_sem=w_recv.at[n],
            device_id=partner, device_id_type=MESH,
        )

    def hop_rows(h):
        return slice(h * toks // 2, (h + 1) * toks // 2)

    def hop_copy(n, h):
        rows = hop_rows(h)
        return pltpu.make_async_remote_copy(
            src_ref=hop_out.at[n, rows, :], dst_ref=hop_in.at[n, rows, :], send_sem=hop_send.at[n, h], recv_sem=hop_recv.at[n, h],
            device_id=after if n == 0 else before, device_id_type=MESH,
        )

    def over(ranges, action):
        def body(i, carry):
            action(i)
            return carry

        for low, high in ranges:
            lax.fori_loop(low, high, body, 0)

    barrier = pltpu.get_barrier_semaphore()

    def greet(i):
        j = i // 4
        zd = z + (j - 3 + j // 4) * sign
        pl.semaphore_signal(barrier, inc=1, device_id=at(x + i % 4, zd), device_id_type=MESH)

    over(((0, SELF), (SELF + 1, NB + 4)), greet)
    for neighbour in (partner, after, before):
        pl.semaphore_signal(barrier, inc=1, device_id=neighbour, device_id_type=MESH)

    def dispatch_copy(ex, i):
        xd, zd = target(i)
        block = (i % 4) * 2 + (zd // 4 + own_half) % 2
        return pltpu.make_async_remote_copy(
            src_ref=sends.at[ex, pl.ds(pl.multiple_of(block * ROWS, ROWS), ROWS), :],
            dst_ref=recvs.at[ex, pl.ds(pl.multiple_of(i * ROWS, ROWS), ROWS), :],
            send_sem=send_sems.at[ex, i],
            recv_sem=recv_sems.at[ex, i],
            device_id=at(xd, zd),
            device_id_type=MESH,
        )

    def back_copy(ex, i):
        xd, zd = origin(i)
        rows = pl.ds(pl.multiple_of(i * ROWS, ROWS), ROWS)
        return pltpu.make_async_remote_copy(
            src_ref=back_sends.at[ex, rows, :],
            dst_ref=back_recvs.at[ex, rows, :],
            send_sem=bsend_sems.at[ex, i],
            recv_sem=brecv_sems.at[ex, i],
            device_id=at(xd, zd),
            device_id_type=MESH,
        )

    def each(copy_of, ex, action, ranges):
        def one(i):
            copy = copy_of(ex, i)
            if action == "start":
                copy.start()
            elif action == "recv":
                copy.wait_recv()
            else:
                copy.wait_send()

        over(ranges, one)

    sub = lax.broadcasted_iota(jnp.int32, (toks, toks), 0)
    lane = lax.broadcasted_iota(jnp.int32, (toks, toks), 1)

    def column(row):
        return jnp.sum(jnp.where(sub == lane, jnp.broadcast_to(row, (toks, toks)), 0), axis=1, keepdims=True)

    def place(ids):
        dx = (ids // 2 - x + XS) % XS
        other = (ids % 2 + own_half) % 2
        return dx, other

    def plan(step):
        row_ids = routes[step : step + 1, :]
        col_ids = column(row_ids)
        same = (col_ids == row_ids).astype(jnp.int32)
        rank_col = jnp.sum(jnp.where(lane < sub, same, 0), axis=1, keepdims=True)
        rank_row = jnp.sum(jnp.where(sub < lane, same, 0), axis=0, keepdims=True)
        dx_row, other_row = place(row_ids)
        block_row = dx_row * 2 + other_row
        slot_row = jnp.where(rank_row < ROWS, block_row * ROWS + rank_row, -1)
        pick = jnp.where(sub == slot_row, 1.0, 0.0).astype(BF16)
        spill_row = jnp.where(rank_row == ROWS, block_row, -1)
        spill_sub = lax.broadcasted_iota(jnp.int32, (16, toks), 0)
        pick_spill = jnp.where(spill_sub == spill_row, 1.0, 0.0).astype(BF16)
        dx_col, other_col = place(col_ids)
        first = jnp.where(other_col == 1, 0, 12) + dx_col
        second = jnp.where(other_col == 1, 2 - twist, 1 + twist) * 4 + dx_col
        plain = rank_col < ROWS
        wide = lax.broadcasted_iota(jnp.int32, (toks, HALF * ROWS), 1)
        narrow = lax.broadcasted_iota(jnp.int32, (toks, HALF), 1)
        puts, put_spills = [], []
        for part in range(2):
            begin = part * HALF
            put, put_spill = 0.0, 0.0
            for block in (first, second):
                inside = (block >= begin) & (block < begin + HALF)
                slot = jnp.where(plain & inside, (block - begin) * ROWS + rank_col, -1)
                put = put + jnp.where(wide == slot, 1.0, 0.0)
                slot = jnp.where(plain, -1, block - begin)
                put_spill = put_spill + jnp.where(narrow == slot, 1.0, 0.0)
            puts.append(put.astype(BF16))
            put_spills.append(put_spill.astype(BF16))
        weight = column(mix[step : step + 1, :])
        return pick, pick_spill, puts, put_spills, weight

    def dot(a, b):
        return jnp.dot(a, b, preferred_element_type=F32)

    def dot_t(a, b):
        return lax.dot_general(a, b, (((1,), (1,)), ((), ())), preferred_element_type=F32)

    def fold_rows(value, buffer):
        for c in range(chunks):
            fold[c // 8, pl.ds(c % 8, 8, stride=8), :] = value[:8, c * LANES : (c + 1) * LANES]
        for c in range(chunks, folds * 8):
            fold[c // 8, pl.ds(c % 8, 8, stride=8), :] = jnp.zeros((8, LANES), F32)
        for b in range(folds):
            buffer[:, width + b * LANES : width + (b + 1) * LANES] = fold[b].astype(BF16)

    def unfold_rows(buffer):
        for b in range(folds):
            fold[b] = buffer[:, width + b * LANES : width + (b + 1) * LANES].astype(F32)
        return jnp.concatenate([fold[c // 8, pl.ds(c % 8, 8, stride=8), :] for c in range(chunks)], axis=1)

    def pack(ex, step_plan, values):
        pick, pick_spill, _, _, _ = step_plan
        buffer = sends.at[ex]
        buffer[:, :width] = dot(pick, values).astype(BF16)
        fold_rows(dot(pick_spill, values), buffer)
        recvs[ex, SELF * ROWS : (SELF + 1) * ROWS, :] = sends[ex, 0:ROWS, :]

    def part_rows(part):
        return slice(part * HALF * ROWS, (part + 1) * HALF * ROWS)

    def arrived(ex, part):
        each(dispatch_copy, ex, "recv", PARTS[part])
        buffer = recvs.at[ex, part_rows(part), :]
        x_all[part, 0 : HALF * ROWS, :] = buffer[:, :width]
        x_all[part, HALF * ROWS : HALF * ROWS + 8, :] = unfold_rows(buffer).astype(BF16)

    def send_back(ex, part, value, start):
        buffer = back_sends.at[ex, part_rows(part), :]
        buffer[:, :width] = value[: HALF * ROWS].astype(BF16)
        fold_rows(value[HALF * ROWS :], buffer)
        if start:
            each(back_copy, ex, "start", PARTS[part])
        if part == 1:
            back_recvs[ex, SELF * ROWS : (SELF + 1) * ROWS, :] = back_sends[ex, SELF * ROWS : (SELF + 1) * ROWS, :]

    def collected(ex, step_plan, then, count):
        _, _, puts, put_spills, weight = step_plan
        total = [0.0] * count
        for part in (1, 0):
            each(back_copy, ex, "recv", PARTS[part])
            if part == 0:
                then()
            buffer = back_recvs.at[ex, part_rows(part), :]
            spill = unfold_rows(buffer).astype(BF16)
            for h in range(count):
                rows = slice(h * toks // count, (h + 1) * toks // count)
                total[h] += dot(puts[part][rows], buffer[:, :width]) + dot(put_spills[part][rows], spill)
                if part == 0:
                    yield rows, weight[rows] * total[h]

    def project(step, part):
        gates[step, part] = dot_t(x_all[part], wg[...])
        uppers[step, part] = dot_t(x_all[part], wu[...])

    def activate(step, part):
        gate = gates[step, part]
        return (gate * jax.nn.sigmoid(gate) * uppers[step, part]).astype(BF16)

    def derive(step, part):
        d_inner = dot_t(x_all[part], wd[...])
        gate = gates[step, part]
        r = jax.nn.sigmoid(gate)
        d_gate = (d_inner * uppers[step, part] * r * (1.0 + gate * (1.0 - r))).astype(BF16)
        d_upper = (d_inner * gate * r).astype(BF16)
        return dot(d_gate, wg[...]) + dot(d_upper, wu[...])

    def inv_scale(values):
        return lax.rsqrt(jnp.mean(values * values, axis=-1, keepdims=True) + EPSILON)

    def normed(hidden):
        values = hidden.astype(F32)
        return (values * inv_scale(values) * gain[...]).astype(BF16)

    def pulled(hidden, grad, d_normed):
        values = hidden.astype(F32)
        r = inv_scale(values)
        scaled = d_normed * gain[...]
        mean = jnp.mean(scaled * values, axis=-1, keepdims=True)
        return grad.astype(F32) + r * scaled - values * (r * r * r * mean)

    plan0 = plan(0)
    pack(0, plan0, normed(tokens[...]))
    pl.semaphore_wait(barrier, NB + 3 + 3)
    weight_copy(0).start()
    weight_copy(1).start()
    each(dispatch_copy, 0, "start", ALL)
    plan1 = plan(1)
    pack(1, plan1, cotangent[...])
    each(dispatch_copy, 1, "start", NEAR)
    for n in range(3):
        weight_local(n).start()
    x_all[:, HALF * ROWS + 8 :, :] = jnp.zeros((2, 8, width), BF16)
    arrived(0, 1)
    arrived(0, 0)
    weight_copy(2).start()
    for n in range(3):
        weight_local(n).wait()
    weight_copy(0).wait_recv()
    weight_copy(1).wait_recv()
    project(0, 0)
    project(0, 1)
    far, near = activate(0, 0), activate(0, 1)
    weight_copy(2).wait_recv()
    each(dispatch_copy, 1, "start", MIDDLE)
    send_back(0, 0, dot(far, wd[...]), True)
    send_back(0, 1, dot(near, wd[...]), True)
    for h, (rows, combined) in enumerate(collected(0, plan0, lambda: each(dispatch_copy, 1, "start", LAST), 2)):
        hop_out[0, rows, :] = (tokens[rows, :].astype(F32) + combined).astype(BF16)
        hop_copy(0, h).start()
    for h in range(2):
        hop_copy(0, h).wait_recv()
        hidden1[hop_rows(h), :] = normed(hop_in[0, hop_rows(h), :])
    pack(2, plan1, hidden1[...])
    hidden1[...] = hop_in[0]
    each(dispatch_copy, 2, "start", ALL)
    arrived(2, 1)
    project(1, 1)
    arrived(1, 1)
    send_back(1, 1, derive(1, 1), True)
    send_back(2, 1, dot(activate(1, 1), wd[...]), False)
    arrived(2, 0)
    each(back_copy, 2, "start", NEAR)
    project(1, 0)
    arrived(1, 0)
    send_back(1, 0, derive(1, 0), True)
    send_back(2, 0, dot(activate(1, 0), wd[...]), False)
    for h, (rows, d_normed) in enumerate(collected(1, plan1, lambda: each(back_copy, 2, "start", LAST), 2)):
        hop_out[1, rows, :] = pulled(hidden1[rows, :], cotangent[rows, :], d_normed).astype(BF16)
        hop_copy(1, h).start()
    for h in range(2):
        hop_copy(1, h).wait_recv()
    pack(3, plan0, hop_in[1])
    each(dispatch_copy, 3, "start", ALL)
    arrived(3, 1)
    send_back(3, 1, derive(0, 1), True)
    arrived(3, 0)
    each(back_copy, 2, "start", MIDDLE)
    send_back(3, 0, derive(0, 0), True)
    for rows, combined in collected(2, plan1, lambda: None, 1):
        final[rows, :] = (hidden1[rows, :].astype(F32) + combined).astype(BF16)
    for rows, d_normed in collected(3, plan0, lambda: None, 1):
        grads[rows, :] = pulled(tokens[rows, :], hop_in[1, rows, :], d_normed).astype(BF16)

    for ex in range(4):
        each(dispatch_copy, ex, "sent", ALL)
        each(back_copy, ex, "sent", ALL)
    for n in range(3):
        weight_copy(n).wait_send()
    for n in range(2):
        for h in range(2):
            hop_copy(n, h).wait_send()


def hand_out(final, grads, final_out, grads_out, sems):
    copies = [
        pltpu.make_async_copy(final, final_out, sems.at[0]),
        pltpu.make_async_copy(grads, grads_out, sems.at[1]),
    ]
    for copy in copies:
        copy.start()
    for copy in copies:
        copy.wait()


def local(tokens, norm_gain, w_gate, w_up, w_down, routes, mix_weights, cotangent):
    toks, width = tokens.shape[1:]
    hid = w_gate.shape[3]
    lanes = width + 3 * LANES
    rows = HALF * (ROWS + 2)
    dma = pltpu.SemaphoreType.DMA
    vmem = pl.BlockSpec(memory_space=pltpu.VMEM)
    anywhere = pl.BlockSpec(memory_space=pl.ANY)
    out = jax.ShapeDtypeStruct((toks, width), BF16)
    final, grads = pl.pallas_call(
        kernel,
        out_shape=(out, out),
        in_specs=[vmem] * 2 + [anywhere] * 3 + [vmem] * 3,
        out_specs=(vmem, vmem),
        scratch_shapes=[
            pltpu.VMEM((2 * hid, width), BF16),
            pltpu.VMEM((2 * hid, width), BF16),
            pltpu.VMEM((2 * hid, width), BF16),
            pltpu.VMEM((4, 8 * ROWS, lanes), BF16),
            pltpu.VMEM((4, NB * ROWS, lanes), BF16),
            pltpu.VMEM((4, NB * ROWS, lanes), BF16),
            pltpu.VMEM((4, NB * ROWS, lanes), BF16),
            pltpu.VMEM((3, HALF * ROWS, LANES), F32),
            pltpu.VMEM((2, rows, width), BF16),
            pltpu.VMEM((2, 2, rows, 2 * hid), F32),
            pltpu.VMEM((2, 2, rows, 2 * hid), F32),
            pltpu.VMEM((toks, width), BF16),
            pltpu.VMEM((2, toks, width), BF16),
            pltpu.VMEM((2, toks, width), BF16),
            dma((4, NB)),
            dma((4, NB)),
            dma((4, NB)),
            dma((4, NB)),
            dma((3,)),
            dma((3,)),
            dma((3,)),
            dma((2, 2)),
            dma((2, 2)),
        ],
        compiler_params=pltpu.CompilerParams(
            collective_id=0, has_side_effects=True, vmem_limit_bytes=56 * 1024 * 1024
        ),
    )(
        tokens[0], norm_gain, w_gate[0, 0].T, w_up[0, 0].T, w_down[0, 0],
        routes[0, :, :, 0], mix_weights[0, :, :, 0], cotangent[0],
    )
    final, grads = pl.pallas_call(
        hand_out,
        out_shape=(out, out),
        in_specs=[anywhere] * 2,
        out_specs=(anywhere, anywhere),
        scratch_shapes=[dma((2,))],
    )(final, grads)
    return final[None], grads[None]


def solution(mesh):
    in_specs = (
        P("section", "expert", None),
        P("section", None),
        P("section", "expert", None, None),
        P("section", "expert", None, None),
        P("section", "expert", None, None),
        P("section", None, "expert", None),
        P("section", None, "expert", None),
        P("section", "expert", None),
    )
    out_specs = (P("section", "expert", None), P("section", "expert", None))
    return jax.shard_map(local, mesh=mesh, in_specs=in_specs, out_specs=out_specs, check_vma=False)
```
